512 devices in a mesh: dp: 128 (over z, x, core), mp: 4 (over y).
Axes of the slice: x: 4, y: 4, z: 16, core: 2. Of those that a mesh axis runs over, the one named last changes fastest.
Arguments:
- session_length: int32 [128], P('dp'), may hold values from 1 to 128
- event_owner: int32 [16384, 1], P('dp'), may hold values from 0 to 127; in each aligned block of 128 rows (0 to 127, 128 to 255, ...) at most 2 rows name the same one
- event_row: int32 [16384], P('dp'), may hold values from 0 to 255
- text_rows: bfloat16 [32768, 4096], P('dp', 'mp'), may hold values from -6 to 6
- image_rows: bfloat16 [32768, 4096], P('dp', 'mp'), may hold values from -6 to 6
- price: float32 [32768], P('dp'), may hold values from 0.2 to 5
- price_dir: bfloat16 [4096], P('mp'), may hold values from -4 to 4
- norm_gain: bfloat16 [4096], P('mp'), may hold values from 0.5 to 1.5
- w_query: bfloat16 [4096, 2048], P('dp', 'mp'), may hold values from -1 to 1
- w_key: bfloat16 [4096, 2048], P('dp', 'mp'), may hold values from -1 to 1
- w_value: bfloat16 [4096, 2048], P('dp', 'mp'), may hold values from -0.09375 to 0.09375
- cotangent: bfloat16 [16384, 4096], P('dp', 'mp'), may hold values from -6 to 6
Outputs:
- context: bfloat16 [16384, 2048], P('dp', 'mp')
- text_grad: float32 [32768, 4096], P('dp', 'mp')
- image_grad: float32 [32768, 4096], P('dp', 'mp')
The draws below stay inside these ranges and needn't reach their ends.
Inputs may be any that keep to these rules, and one draw needn't show every extreme that they name: `event_owner`: among the event slots of one index of dp, no owner is named more than 2 times, a bound that some block reaches.
All inputs are finite; a program needn't handle non-finite values.
Results may differ from the reference program's by a relative error of at most 0.0063.
Values may be sent and summed in bfloat16 or wider, within the bound.
No kernel may reach another device: no remote copies, remote signals or barrier semaphores. Data moves between devices by JAX's collectives and lax.ppermute only.
A program may use at most 64 MiB of HBM per device.

```python
import math
import jax
import jax.numpy as jnp
import numpy as np
from jax import lax

D = 4096
HEADS = 16
HD = 128
SLOT = 128
ITEMS_DEV = 256
QW = 2048
TOK_DEV = 128
SESSIONS = 128
TOKENS = 16384
ITEMS = 32768
CAP = 2
N_DP = 128


def projection_parts(key):
    base_part = jax.random.normal(jax.random.fold_in(key, 11), (D, HEADS * HD), jnp.float32) / math.sqrt(D)
    other_part = jax.random.normal(jax.random.fold_in(key, 12), (D, HEADS * HD), jnp.float32) / math.sqrt(D)
    return (base_part, other_part)


def draw_w_query(key, part):
    base_part, other_part = projection_parts(key)
    return jnp.clip(base_part, -1.0, 1.0).astype(jnp.bfloat16)


def draw_w_key(key, part):
    base_part, other_part = projection_parts(key)
    return jnp.clip(other_part, -1.0, 1.0).astype(jnp.bfloat16)


def place_ends(drawn, own_key, smallest, high):
    longest = drawn.shape.index(max(drawn.shape))
    spots = []
    for shift in (0, 1):
        where = [jax.random.randint(jax.random.fold_in(own_key, axis), (), 0, length) for axis, length in enumerate(drawn.shape)]
        where[longest] = (where[longest] + shift) % drawn.shape[longest]
        spots.append(tuple(where))
    return drawn.at[spots[0]].set(smallest).at[spots[1]].set(high)


def shard_levels(key, dims, pieces, smallest, largest):
    def one(axis_at, shards_of):
        heights = jax.random.uniform(jax.random.fold_in(jax.random.fold_in(key, 6), axis_at), (shards_of,), jnp.float32, smallest / len(pieces), largest / len(pieces))
        return jnp.repeat(jnp.exp(heights), dims[axis_at] // shards_of).reshape((-1,) + (1,) * (len(dims) - axis_at - 1))

    factor_of = one(*pieces[0])
    for cut in pieces[1:]:
        factor_of = factor_of * one(*cut)
    return factor_of


def assign_block(own_key, own, number, rows, count, top, most, slope):
    sequence = jax.random.permutation(own_key, count)
    heavy_load, ordinary = load_shares(count, rows * top, most, slope, True), load_shares(count, rows * top, most, slope, False)
    places = jnp.arange(count)

    def named(lengths, turn):
        used = int((lengths > 0).sum())
        fixed = max(1, used // 4)
        passed = fixed + (places - fixed + turn * (used - fixed)) % max(1, count - fixed)
        return jnp.zeros((count,), jnp.int32).at[sequence[jnp.where(places < fixed, places, passed)]].set(jnp.asarray(lengths, jnp.int32))

    lengths = jnp.where(number % 4 == 0, named(heavy_load, number // 4), named(ordinary, number - number // 4 - 1))
    mixed = jax.random.permutation(jax.random.fold_in(own, 3), count)
    donor, receiver = mixed[0:count // 2 * 2:2], mixed[1:count // 2 * 2:2]
    slack = jnp.minimum(lengths[donor] - 1, most - lengths[receiver]) // 2
    slack = jnp.where((donor == sequence[0]) | (receiver == sequence[0]) | (lengths[receiver] == 0), 0, jnp.maximum(slack, 0))
    passed = jax.random.randint(jax.random.fold_in(own, 4), (count // 2,), 0, 1 << 20) % (slack + 1)
    lengths = lengths.at[donor].add(-passed).at[receiver].add(passed)
    members = jnp.searchsorted(jnp.cumsum(lengths), jnp.arange(rows * top), side="right").astype(jnp.int32)
    listing = members.reshape(top, rows).T
    listing = listing[jax.random.permutation(jax.random.fold_in(own, 1), rows)]
    turn = jax.random.randint(jax.random.fold_in(own, 2), (rows, 1), 0, top)
    return jnp.take_along_axis(listing, (jnp.arange(top)[None, :] + turn) % top, axis=1)


def load_shares(count, total, most, skew, full):
    weights = [(1 << 20) // math.isqrt(rank ** skew) + 1 for rank in range(1, count + 1)]
    largest = most if full else min(most, max(-(-total // count), total * weights[0] // sum(weights)))
    least = 1 if total - largest >= count - 1 else 0
    given, rest = [largest] + [least] * (count - 1), total - largest - least * (count - 1)
    while rest > 0:
        movable = [i for i in range(1, count) if given[i] < largest] or [i for i in range(1, count) if given[i] < most]
        pool, left = sum([weights[i] for i in movable]), rest
        for i in movable:
            more = min(most - given[i], max(1, left * weights[i] // pool), rest)
            given[i] = given[i] + more
            rest = rest - more
    return np.array(given)


def noise(rng, dims, deviation, most, pieces=(), kind=jnp.bfloat16):
    values = deviation * jax.random.normal(rng, dims, jnp.float32)
    if pieces:
        values = values * shard_levels(rng, dims, pieces, -0.22, 0.18)
    return jnp.clip(values, -most, most).astype(kind)


def setup_inputs(seed: int = 0) -> dict:
    splits = jax.random.split(jax.random.key(seed), 13)
    session_length = place_ends(jax.random.randint(splits[0], (SESSIONS,), 1, SLOT + 1), jax.random.fold_in(splits[0], 1), 1, SLOT).astype(jnp.int32)
    event_owner_keys = jax.random.split(jax.random.fold_in(splits[1], 1), TOKENS // TOK_DEV)
    event_owner_turns = jax.random.permutation(jax.random.fold_in(splits[1], 3), TOKENS // TOK_DEV)
    event_owner = jax.vmap(lambda own, number: assign_block(jax.random.fold_in(splits[1], 2), own, number, TOK_DEV, N_DP, 1, CAP, 2))(event_owner_keys, event_owner_turns).reshape((TOKENS, 1))
    event_row = place_ends(jax.random.randint(splits[2], (TOKENS,), 0, ITEMS_DEV), jax.random.fold_in(splits[2], 1), 0, ITEMS_DEV - 1).astype(jnp.int32)
    text_rows = noise(splits[3], (ITEMS, D), 1.0, 6.0, ((0, 128), (1, 4)))
    image_rows = noise(splits[4], (ITEMS, D), 1.0, 6.0, ((0, 128), (1, 4)))
    price = jnp.clip(jnp.exp(math.log(5.0) - 3.218876 * jax.random.uniform(splits[5], (ITEMS,), jnp.float32) ** shard_levels(splits[5], (ITEMS,), ((0, 128),), -0.2, 0.2)), 0.2, 5.0)
    price_dir = noise(splits[6], (D,), 1.0, 4.0, ((0, 4),))
    norm_gain = jnp.clip(1.0 + 0.1 * jax.random.normal(splits[7], (D,), jnp.float32), 0.5, 1.5).astype(jnp.bfloat16)
    w_query = draw_w_query(jax.random.fold_in(splits[12], 71), 0)
    w_key = draw_w_key(jax.random.fold_in(splits[12], 71), 0)
    w_value = noise(splits[10], (D, QW), D ** -0.5, 0.09375, ((0, 128), (1, 4)))
    cotangent = noise(splits[11], (TOKENS, D), 1.0, 6.0, ((0, 128), (1, 4)))
    return {"session_length": session_length, "event_owner": event_owner, "event_row": event_row, "text_rows": text_rows, "image_rows": image_rows, "price": price, "price_dir": price_dir, "norm_gain": norm_gain, "w_query": w_query, "w_key": w_key, "w_value": w_value, "cotangent": cotangent}


def one_session(session_args, text_rows, image_rows, price, price_dir, norm_gain, w_query, w_key, w_value):
    items, length = session_args
    text_got = text_rows[items].astype(jnp.float32)
    image_got = image_rows[items].astype(jnp.float32)
    joined_rows = (text_got * image_got + price[items][:, None] * price_dir.astype(jnp.float32)[None, :]).astype(jnp.bfloat16)
    joined_float = joined_rows.astype(jnp.float32)
    scale = lax.rsqrt(lax.optimization_barrier(jnp.mean(joined_float * joined_float, axis=1, keepdims=True)) + 1e-06)
    normed = (joined_float * scale * norm_gain.astype(jnp.float32)[None, :]).astype(jnp.bfloat16)
    query = jnp.dot(normed, w_query, preferred_element_type=jnp.float32).astype(jnp.bfloat16)
    keys = jnp.dot(normed, w_key, preferred_element_type=jnp.float32).astype(jnp.bfloat16)
    values = jnp.dot(normed, w_value, preferred_element_type=jnp.float32).astype(jnp.bfloat16)
    shape3 = (SLOT, HEADS, HD)
    scores = jnp.einsum('qhd,khd->hqk', query.reshape(shape3).astype(jnp.float32), keys.reshape(shape3).astype(jnp.float32)) / math.sqrt(HD)
    position = jnp.arange(SLOT, dtype=jnp.int32)
    live_mask = position < length
    allowed = (position[None, :] <= position[:, None])[None, :, :] & live_mask[None, None, :]
    scores = jnp.where(allowed, scores, jnp.float32(-1e+30))
    row_max = lax.optimization_barrier(jnp.max(scores, axis=-1, keepdims=True))
    powers = jnp.exp(scores - row_max)
    probs = (powers / lax.optimization_barrier(jnp.sum(powers, axis=-1, keepdims=True))).astype(jnp.bfloat16)
    context = jnp.einsum('hqk,khd->qhd', probs.astype(jnp.float32), values.reshape(shape3).astype(jnp.float32))
    context = jnp.where(live_mask[:, None, None], context, jnp.float32(0.0))
    return context.reshape(SLOT, HEADS * HD).astype(jnp.bfloat16)

def reference(session_length, event_owner, event_row, text_rows, image_rows, price, price_dir, norm_gain, w_query, w_key, w_value, cotangent):
    item = (event_owner[:, 0] * ITEMS_DEV + event_row).astype(jnp.int32)

    def per_session(session_args):
        return one_session(session_args, text_rows, image_rows, price, price_dir, norm_gain, w_query, w_key, w_value)
    context = lax.map(per_session, (item.reshape(SESSIONS, SLOT), session_length))
    context = context.reshape(TOKENS, HEADS * HD)
    grad_float = cotangent.astype(jnp.float32)
    text_grad = jnp.zeros((ITEMS, D), jnp.float32).at[item].add(grad_float * image_rows[item].astype(jnp.float32))
    image_grad = jnp.zeros((ITEMS, D), jnp.float32).at[item].add(grad_float * text_rows[item].astype(jnp.float32))
    return (context, text_grad, image_grad)
```

```python
import math

import jax
import jax.numpy as jnp
from jax import lax
from jax.sharding import PartitionSpec as P

HD = 128
SLOT = 128


def one_hot(rows, columns):
    return (rows[:, None] == columns[None, :]).astype(jnp.bfloat16)


def pick(selector, values):
    return jnp.dot(selector, values, preferred_element_type=jnp.float32)


def attend(query, keys, values, session_length):
    heads_here = query.shape[1] // HD
    shape3 = (SLOT, heads_here, HD)
    scores = jnp.einsum(
        "qhd,khd->hqk",
        query.reshape(shape3),
        keys.reshape(shape3),
        preferred_element_type=jnp.float32,
    ) / math.sqrt(HD)
    position = jnp.arange(SLOT, dtype=jnp.int32)
    live_mask = position < session_length[0]
    allowed = (position[None, :] <= position[:, None])[None] & live_mask[None, None, :]
    scores = jnp.where(allowed, scores, jnp.float32(-1e30))
    row_max = jnp.max(scores, axis=-1, keepdims=True)
    powers = jnp.exp(scores - row_max)
    probs = (powers / jnp.sum(powers, axis=-1, keepdims=True)).astype(jnp.bfloat16)
    context = jnp.einsum(
        "hqk,khd->qhd", probs, values.reshape(shape3), preferred_element_type=jnp.float32
    )
    context = jnp.where(live_mask[:, None, None], context, jnp.float32(0.0))
    return context.reshape(SLOT, heads_here * HD).astype(jnp.bfloat16)


def local(
    session_length,
    event_owner,
    event_row,
    text_rows,
    image_rows,
    price,
    price_dir,
    norm_gain,
    w_query,
    w_key,
    w_value,
    cotangent,
):
    peers = lax.axis_size("dp")
    parts = lax.axis_size("mp")
    mine = lax.axis_index("mp")
    tok_count = event_row.shape[0]
    capacity = 2 * tok_count // peers
    col_width = text_rows.shape[1]
    table_rows = text_rows.shape[0]
    slots = jnp.arange(peers * capacity, dtype=jnp.int32)

    weights = lax.all_gather(
        jnp.concatenate([w_query, w_key, w_value], axis=1), "dp", axis=0, tiled=True
    )

    owner_ids = event_owner[:, 0]
    place = jnp.arange(tok_count, dtype=jnp.int32)
    same = (owner_ids[:, None] == owner_ids[None, :]) & (place[None, :] < place[:, None])
    slot_ids = owner_ids * capacity + jnp.sum(same.astype(jnp.int32), axis=1)
    taken = slots[:, None] == slot_ids[None, :]
    requests = (
        jnp.sum(jnp.where(taken, event_row[None, :] + 1, 0), axis=1) - 1
    ).reshape(peers, capacity)
    got_ids = lax.all_to_all(requests, "dp", split_axis=0, concat_axis=0, tiled=True).reshape(-1)

    text_float = text_rows.astype(jnp.float32)
    image_float = image_rows.astype(jnp.float32)
    table = (
        text_float * image_float + price[:, None] * price_dir.astype(jnp.float32)[None, :]
    ).astype(jnp.bfloat16)
    wanted = one_hot(got_ids, jnp.arange(table_rows, dtype=jnp.int32))
    replies = lax.all_to_all(
        pick(wanted, table).astype(jnp.bfloat16).reshape(peers, capacity, col_width),
        "dp",
        split_axis=0,
        concat_axis=0,
        tiled=True,
    ).reshape(peers * capacity, col_width)

    grad_buffer = pick(taken.astype(jnp.bfloat16), cotangent).astype(jnp.bfloat16)
    grad_buffer, replies = lax.optimization_barrier((grad_buffer, replies))
    got_grads = lax.all_to_all(
        grad_buffer.reshape(peers, capacity, col_width),
        "dp",
        split_axis=0,
        concat_axis=0,
        tiled=True,
    ).reshape(peers * capacity, col_width)
    row_sums = pick(wanted.T, got_grads)
    text_grad = row_sums * image_float
    image_grad = row_sums * text_float

    joined = pick(one_hot(slot_ids, slots), replies).astype(jnp.bfloat16)
    turns = [
        joined if k == 0 else lax.ppermute(joined, "mp", [(i, (i + k) % parts) for i in range(parts)])
        for k in range(parts)
    ]
    stacked = jnp.stack(turns)
    features = jnp.concatenate(
        [
            lax.dynamic_index_in_dim(stacked, (mine - s) % parts, 0, keepdims=False)
            for s in range(parts)
        ],
        axis=1,
    ).astype(jnp.float32)
    gain = lax.all_gather(norm_gain, "mp", axis=0, tiled=True).astype(jnp.float32)
    scale = lax.rsqrt(jnp.mean(features * features, axis=1, keepdims=True) + 1e-06)
    normed = (features * scale * gain[None, :]).astype(jnp.bfloat16)
    projected = jnp.dot(normed, weights, preferred_element_type=jnp.float32).astype(jnp.bfloat16)
    width = w_query.shape[1]
    context = attend(
        projected[:, :width],
        projected[:, width : 2 * width],
        projected[:, 2 * width :],
        session_length,
    )
    return (context, text_grad, image_grad)


def solution(mesh):
    return jax.shard_map(
        local,
        mesh=mesh,
        in_specs=(
            P("dp"),
            P("dp", None),
            P("dp"),
            P("dp", "mp"),
            P("dp", "mp"),
            P("dp"),
            P("mp"),
            P("mp"),
            P("dp", "mp"),
            P("dp", "mp"),
            P("dp", "mp"),
            P("dp", "mp"),
        ),
        out_specs=(P("dp", "mp"), P("dp", "mp"), P("dp", "mp")),
        check_vma=False,
    )
```

```python
import math

import jax
import jax.numpy as jnp
from jax import lax
from jax.experimental import pallas as pl
from jax.experimental.pallas import tpu as pltpu
from jax.sharding import Mesh
from jax.sharding import PartitionSpec as P

HD = 128
GAIN_ROWS = 8
DP = ("zh", "zl", "x", "c")


def one_hot(rows, columns):
    return (rows[:, None] == columns[None, :]).astype(jnp.bfloat16)


def pick(selector, values):
    return jnp.dot(selector, values, preferred_element_type=jnp.float32)


def select_kernel(slot_ref, replies_ref, gain_ref, out_ref):
    tok_count, slot_count = slot_ref.shape[0], replies_ref.shape[0]
    slots = lax.broadcasted_iota(jnp.int32, (tok_count, slot_count), 1)
    chosen = (slot_ref[...] == slots).astype(jnp.bfloat16)
    out_ref[:tok_count, :] = pick(chosen, replies_ref[...]).astype(jnp.bfloat16)
    out_ref[tok_count:, :] = jnp.broadcast_to(
        gain_ref[...], (out_ref.shape[0] - tok_count, gain_ref.shape[1])
    )


def select(slot_ids, replies, gain):
    tok_count, col_width = slot_ids.shape[0], replies.shape[1]
    return pl.pallas_call(
        select_kernel,
        out_shape=jax.ShapeDtypeStruct((tok_count + GAIN_ROWS, col_width), jnp.bfloat16),
        name="select",
    )(slot_ids.reshape(tok_count, 1), replies, gain.reshape(1, col_width))


def project_kernel(
    order_ref, length_ref, f0, f1, f2, f3, w_ref, out_ref, acc_ref, normed_ref
):
    step = pl.program_id(0)
    tok_count, width = out_ref.shape
    parts = (f0, f1, f2, f3)

    @pl.when(step == 0)
    def _():
        total = jnp.zeros((tok_count, 1), jnp.float32)
        for part in parts:
            value = part[:tok_count, :].astype(jnp.float32)
            total = total + jnp.sum(value * value, axis=1, keepdims=True)
        scale = lax.rsqrt(total / (len(parts) * f0.shape[1]) + 1e-06)
        for k, part in enumerate(parts):
            gain = part[tok_count : tok_count + 1, :].astype(jnp.float32)
            value = part[:tok_count, :].astype(jnp.float32)
            normed_ref[k] = (value * scale * gain).astype(jnp.bfloat16)

    weights = w_ref[...].reshape(normed_ref.shape[2], 3 * width)
    product = jnp.dot(normed_ref[step], weights, preferred_element_type=jnp.float32)

    @pl.when(step == 0)
    def _():
        acc_ref[...] = product

    @pl.when(step > 0)
    def _():
        acc_ref[...] += product

    @pl.when(step == pl.num_programs(0) - 1)
    def _():
        length = length_ref[0]
        row = lax.broadcasted_iota(jnp.int32, (tok_count, tok_count), 0)
        column = lax.broadcasted_iota(jnp.int32, (tok_count, tok_count), 1)
        allowed = (column <= row) & (column < length)
        live = lax.broadcasted_iota(jnp.int32, (tok_count, HD), 0) < length
        for at in range(0, width, HD):
            query, keys, values = (
                acc_ref[:, k * width + at : k * width + at + HD].astype(jnp.bfloat16)
                for k in range(3)
            )
            scores = lax.dot_general(
                query, keys, (((1,), (1,)), ((), ())), preferred_element_type=jnp.float32
            ) / math.sqrt(HD)
            scores = jnp.where(allowed, scores, jnp.float32(-1e30))
            powers = jnp.exp(scores - jnp.max(scores, axis=-1, keepdims=True))
            probs = (powers / jnp.sum(powers, axis=-1, keepdims=True)).astype(jnp.bfloat16)
            context = jnp.dot(probs, values, preferred_element_type=jnp.float32)
            out_ref[:, at : at + HD] = jnp.where(live, context, 0.0).astype(jnp.bfloat16)


def project_and_attend(order, session_length, turns, weights):
    rows, col_width = turns[0].shape
    tok_count = rows - GAIN_ROWS
    inner, quarters, depth, columns = weights.shape
    whole = pl.BlockSpec((rows, col_width), lambda s, order, length: (0, 0))
    return pl.pallas_call(
        project_kernel,
        out_shape=jax.ShapeDtypeStruct((tok_count, columns // 3), jnp.bfloat16),
        grid_spec=pltpu.PrefetchScalarGridSpec(
            num_scalar_prefetch=2,
            grid=(quarters,),
            in_specs=[whole] * 4
            + [
                pl.BlockSpec(
                    (inner, 1, depth, columns), lambda s, order, length: (0, order[s], 0, 0)
                )
            ],
            out_specs=pl.BlockSpec(
                (tok_count, columns // 3), lambda s, order, length: (0, 0)
            ),
            scratch_shapes=[
                pltpu.VMEM((tok_count, columns), jnp.float32),
                pltpu.VMEM((quarters, tok_count, col_width), jnp.bfloat16),
            ],
        ),
        compiler_params=pltpu.CompilerParams(vmem_limit_bytes=56 * 1024 * 1024),
        name="project_and_attend",
    )(order, session_length, *turns, weights)


def local(
    session_length,
    event_owner,
    event_row,
    text_rows,
    image_rows,
    price,
    price_dir,
    norm_gain,
    w_query,
    w_key,
    w_value,
    cotangent,
):
    peers = lax.axis_size(DP)
    parts = lax.axis_size("mp")
    mine = lax.axis_index("mp")
    tok_count = event_row.shape[0]
    capacity = 2 * tok_count // peers
    col_width = text_rows.shape[1]
    table_rows = text_rows.shape[0]
    slots = jnp.arange(peers * capacity, dtype=jnp.int32)

    quarter = lax.all_gather(
        jnp.concatenate([w_query, w_key, w_value], axis=1), "zh", axis=0, tiled=True
    )
    weights = lax.all_gather(quarter, ("zl", "x", "c"), axis=0, tiled=True).reshape(
        -1, lax.axis_size("zh"), *w_query.shape[:1], 3 * w_query.shape[1]
    )

    owner_ids = event_owner[:, 0]
    place = jnp.arange(tok_count, dtype=jnp.int32)
    same = (owner_ids[:, None] == owner_ids[None, :]) & (place[None, :] < place[:, None])
    slot_ids = owner_ids * capacity + jnp.sum(same.astype(jnp.int32), axis=1)
    taken = slots[:, None] == slot_ids[None, :]
    requests = (
        jnp.sum(jnp.where(taken, event_row[None, :] + 1, 0), axis=1) - 1
    ).reshape(peers, capacity)
    requests, _ = lax.optimization_barrier((requests, quarter))
    got_ids = lax.all_to_all(requests, DP, split_axis=0, concat_axis=0, tiled=True).reshape(-1)

    text_float = text_rows.astype(jnp.float32)
    image_float = image_rows.astype(jnp.float32)
    table = (
        text_float * image_float + price[:, None] * price_dir.astype(jnp.float32)[None, :]
    ).astype(jnp.bfloat16)
    wanted = one_hot(got_ids, jnp.arange(table_rows, dtype=jnp.int32))
    replies = lax.all_to_all(
        pick(wanted, table).astype(jnp.bfloat16).reshape(peers, capacity, col_width),
        DP,
        split_axis=0,
        concat_axis=0,
        tiled=True,
    ).reshape(peers * capacity, col_width)

    grad_buffer = pick(taken.astype(jnp.bfloat16), cotangent).astype(jnp.bfloat16)
    grad_buffer, replies = lax.optimization_barrier((grad_buffer, replies))
    got_grads = lax.all_to_all(
        grad_buffer.reshape(peers, capacity, col_width),
        DP,
        split_axis=0,
        concat_axis=0,
        tiled=True,
    ).reshape(peers * capacity, col_width)
    row_sums = pick(wanted.T, got_grads)
    text_grad = row_sums * image_float
    image_grad = row_sums * text_float

    joined = select(slot_ids, replies, norm_gain)
    turns = [
        joined if k == 0 else lax.ppermute(joined, "mp", [(i, (i + k) % parts) for i in range(parts)])
        for k in range(parts)
    ]
    order = (mine - jnp.arange(parts, dtype=jnp.int32)) % parts
    context = project_and_attend(order, session_length, turns, weights)
    return (context, text_grad, image_grad)


def solution(mesh):
    fine = Mesh(mesh.devices.reshape(4, -1, 4, 2, mesh.shape["mp"]), (*DP, "mp"))
    return jax.shard_map(
        local,
        mesh=fine,
        in_specs=(
            P(DP),
            P(DP, None),
            P(DP),
            P(DP, "mp"),
            P(DP, "mp"),
            P(DP),
            P("mp"),
            P("mp"),
            P(DP, "mp"),
            P(DP, "mp"),
            P(DP, "mp"),
            P(DP, "mp"),
        ),
        out_specs=(P(DP, "mp"), P(DP, "mp"), P(DP, "mp")),
        check_vma=False,
    )
```

```python
import math

import jax
import jax.numpy as jnp
from jax import lax
from jax.experimental import pallas as pl
from jax.experimental.pallas import tpu as pltpu
from jax.sharding import Mesh
from jax.sharding import PartitionSpec as P

HD = 128
GAIN_ROWS = 8
XS = 4
CS = 2
DP = ("z", "x", "c")


def pick(selector, values):
    return jnp.dot(selector, values, preferred_element_type=jnp.float32)


def iota(shape, axis):
    return lax.broadcasted_iota(jnp.int32, shape, axis)


def answer_kernel(ids_ref, table_ref, out_ref):
    count, table_rows = ids_ref.shape[1], table_ref.shape[0]
    width = table_ref.shape[1] // XS
    group = 2 * XS * CS
    target = iota((count, count), 0)
    source = iota((count, count), 1)
    at = lax.rem(target, group)
    moved = (
        target - at + lax.rem(at // 2, XS) * (2 * CS) + (at // (2 * XS)) * 2 + lax.rem(at, 2)
    )
    ids = jnp.sum(
        jnp.where(moved == source, ids_ref[...].astype(jnp.float32), 0.0), axis=1, keepdims=True
    ).astype(jnp.int32)
    wanted = (ids == iota((count, table_rows), 1)).astype(jnp.bfloat16)
    for block in range(XS):
        rows = pick(wanted, table_ref[:, block * width : (block + 1) * width]).astype(
            jnp.bfloat16
        )
        for z in range(count // group):
            to = (z * XS + block) * group
            out_ref[to : to + group, :] = rows[z * group : (z + 1) * group, :]


def answer(ids, table):
    count, columns = ids.shape[0], table.shape[1]
    return pl.pallas_call(
        answer_kernel,
        out_shape=jax.ShapeDtypeStruct((count * XS, columns // XS), jnp.bfloat16),
        name="answer",
    )(ids.reshape(1, count), table)


def select_kernel(code_ref, replies_ref, gain_ref, out_ref):
    tokens = code_ref.shape[0]
    chosen = (code_ref[...] == iota((tokens, replies_ref.shape[0]), 1)).astype(jnp.bfloat16)
    out_ref[:tokens, :] = pick(chosen, replies_ref[...]).astype(jnp.bfloat16)
    out_ref[tokens:, :] = jnp.broadcast_to(gain_ref[...], (GAIN_ROWS, gain_ref.shape[1]))


def select(codes, replies, gain):
    tokens, width = codes.shape[0], replies.shape[1]
    return pl.pallas_call(
        select_kernel,
        out_shape=jax.ShapeDtypeStruct((tokens + GAIN_ROWS, width), jnp.bfloat16),
        name="select",
    )(codes.reshape(tokens, 1), replies, gain.reshape(1, width))


def project_kernel(order_ref, f0, f1, f2, f3, w_ref, own_ref, s1, s2, s3, acc_ref, normed_ref, sum_ref):
    step = pl.program_id(0)
    tokens = acc_ref.shape[0] // XS
    columns = acc_ref.shape[1]

    @pl.when(step == 0)
    def _():
        total = jnp.zeros((XS * tokens, 1), jnp.float32)
        for k, part in enumerate((f0, f1, f2, f3)):
            value = part[: XS * tokens, :].astype(jnp.float32)
            gain = part[XS * tokens : XS * tokens + 1, :].astype(jnp.float32)
            total = total + jnp.sum(value * value, axis=1, keepdims=True)
            normed_ref[k] = (value * gain).astype(jnp.bfloat16)
        sum_ref[...] = jnp.broadcast_to(total, sum_ref.shape)

    product = pick(normed_ref[step], w_ref[...])

    @pl.when(step == 0)
    def _():
        acc_ref[...] = product

    @pl.when(step > 0)
    def _():
        acc_ref[...] += product

    @pl.when(step == pl.num_programs(0) - 1)
    def _():
        mine = order_ref[XS]
        lane = iota((tokens, HD), 1)
        here = pl.ds(pl.multiple_of(mine * tokens, tokens), tokens)
        own_ref[:, :columns] = acc_ref[here, :]
        own_ref[:, columns:] = sum_ref[here, :]
        for k, out_ref in ((1, s1), (2, s2), (3, s3)):
            there = pl.ds(pl.multiple_of(lax.rem(mine + k, XS) * tokens, tokens), tokens)
            out_ref[:, :columns] = acc_ref[there, :].astype(jnp.bfloat16)
            total = sum_ref[there, :]
            high = total.astype(jnp.bfloat16).astype(jnp.float32)
            middle = (total - high).astype(jnp.bfloat16).astype(jnp.float32)
            low = total - high - middle
            out_ref[:, columns:] = jnp.where(
                lane == 0, high, jnp.where(lane == 1, middle, low)
            ).astype(jnp.bfloat16)


def project(order, turns, weights):
    rows, width = turns[0].shape
    tokens = (rows - GAIN_ROWS) // XS
    columns = weights.shape[1]
    whole = pl.BlockSpec((rows, width), lambda s, order: (0, 0))
    out = pl.BlockSpec((tokens, columns + HD), lambda s, order: (0, 0))
    return pl.pallas_call(
        project_kernel,
        out_shape=[jax.ShapeDtypeStruct((tokens, columns + HD), jnp.float32)]
        + [jax.ShapeDtypeStruct((tokens, columns + HD), jnp.bfloat16)] * 3,
        grid_spec=pltpu.PrefetchScalarGridSpec(
            num_scalar_prefetch=1,
            grid=(len(turns),),
            in_specs=[whole] * 4 + [pl.BlockSpec((width, columns), lambda s, order: (order[s], 0))],
            out_specs=[out] * 4,
            scratch_shapes=[
                pltpu.VMEM((XS * tokens, columns), jnp.float32),
                pltpu.VMEM((len(turns), XS * tokens, width), jnp.bfloat16),
                pltpu.VMEM((XS * tokens, HD), jnp.float32),
            ],
        ),
        compiler_params=pltpu.CompilerParams(vmem_limit_bytes=32 * 1024 * 1024),
        name="project",
    )(order, *turns, weights)


def attend_kernel(length_ref, own_ref, p1, p2, p3, out_ref):
    tokens, width = out_ref.shape
    columns = 3 * width
    total = own_ref[:, columns : columns + 1]
    for part in (p1, p2, p3):
        pieces = part[:, columns : columns + HD].astype(jnp.float32)
        total = total + ((pieces[:, 0:1] + pieces[:, 1:2]) + pieces[:, 2:3])
    scale = lax.rsqrt(total / (8 * width) + 1e-06)
    length = length_ref[0]
    row = iota((tokens, tokens), 0)
    column = iota((tokens, tokens), 1)
    allowed = (column <= row) & (column < length)
    live = iota((tokens, HD), 0) < length
    for at in range(0, width, HD):
        query, keys, values = (
            (
                (
                    own_ref[:, a : a + HD]
                    + p1[:, a : a + HD].astype(jnp.float32)
                    + p2[:, a : a + HD].astype(jnp.float32)
                    + p3[:, a : a + HD].astype(jnp.float32)
                )
                * scale
            ).astype(jnp.bfloat16)
            for a in (at, width + at, 2 * width + at)
        )
        scores = lax.dot_general(
            query, keys, (((1,), (1,)), ((), ())), preferred_element_type=jnp.float32
        ) / math.sqrt(HD)
        scores = jnp.where(allowed, scores, jnp.float32(-1e30))
        powers = jnp.exp(scores - jnp.max(scores, axis=-1, keepdims=True))
        probs = (powers / jnp.sum(powers, axis=-1, keepdims=True)).astype(jnp.bfloat16)
        context = pick(probs, values)
        out_ref[:, at : at + HD] = jnp.where(live, context, 0.0).astype(jnp.bfloat16)


def attend(session_length, own, parts):
    tokens, columns = own.shape
    vmem = pl.BlockSpec(memory_space=pltpu.VMEM)
    return pl.pallas_call(
        attend_kernel,
        out_shape=jax.ShapeDtypeStruct((tokens, (columns - HD) // 3), jnp.bfloat16),
        in_specs=[pl.BlockSpec(memory_space=pltpu.SMEM)] + [vmem] * 4,
        out_specs=vmem,
        name="attend",
    )(session_length, own, *parts)


def turn(value, axis, k):
    size = lax.axis_size(axis)
    return lax.ppermute(value, axis, [(i, (i + k) % size) for i in range(size)])


def exchange(value):
    return lax.all_to_all(value, DP, split_axis=0, concat_axis=0, tiled=True)


def local(
    session_length,
    event_owner,
    event_row,
    text_rows,
    image_rows,
    price,
    price_dir,
    norm_gain,
    w_query,
    w_key,
    w_value,
    cotangent,
):
    peers = lax.axis_size(DP)
    parts = lax.axis_size("mp")
    mine, across = lax.axis_index("mp"), lax.axis_index("x")
    tok_count = event_row.shape[0]
    capacity = 2 * tok_count // peers
    table_rows, col_width = text_rows.shape
    slots = jnp.arange(peers * capacity, dtype=jnp.int32)
    block = CS * w_query.shape[0]

    weights = lax.all_gather(
        jnp.concatenate([w_query, w_key, w_value], axis=1), ("z", "c"), axis=0, tiled=True
    )

    owner_ids = event_owner[:, 0]
    place = jnp.arange(tok_count, dtype=jnp.int32)
    same = (owner_ids[:, None] == owner_ids[None, :]) & (place[None, :] < place[:, None])
    earlier = jnp.sum(same.astype(jnp.int32), axis=1)
    slot_ids = owner_ids * capacity + earlier
    taken = slots[:, None] == slot_ids[None, :]
    requests = (
        jnp.sum(jnp.where(taken, event_row[None, :] + 1, 0), axis=1) - 1
    ).reshape(peers, capacity)
    got_ids = exchange(requests).reshape(-1)

    codes = lax.all_gather(owner_ids * (XS * capacity) + earlier, "x", axis=0)
    codes = (codes + capacity * jnp.arange(XS, dtype=jnp.int32)[:, None]).reshape(-1)

    text_float = text_rows.astype(jnp.float32)
    image_float = image_rows.astype(jnp.float32)
    table = (
        text_float * image_float + price[:, None] * price_dir.astype(jnp.float32)[None, :]
    ).astype(jnp.bfloat16)
    table = (
        table.reshape(table_rows, -1, XS, block).transpose(0, 2, 1, 3).reshape(table_rows, col_width)
    )
    got_ids, table, codes = lax.optimization_barrier((got_ids, table, codes))
    replies = exchange(
        answer(got_ids, table).reshape(peers, XS * capacity, col_width // XS)
    ).reshape(peers * XS * capacity, col_width // XS)

    grad_buffer = pick(taken.astype(jnp.bfloat16), cotangent).astype(jnp.bfloat16)
    grad_buffer, replies = lax.optimization_barrier((grad_buffer, replies))
    got_grads = exchange(grad_buffer.reshape(peers, capacity, col_width)).reshape(
        peers * capacity, col_width
    )
    wanted = (jnp.arange(table_rows, dtype=jnp.int32)[:, None] == got_ids[None, :]).astype(
        jnp.bfloat16
    )
    row_sums = pick(wanted, got_grads)
    text_grad = row_sums * image_float
    image_grad = row_sums * text_float

    gain = lax.dynamic_index_in_dim(
        norm_gain.reshape(-1, XS, block), across, 1, keepdims=False
    ).reshape(-1)
    joined = select(codes, replies, gain)
    turns = [joined] + [turn(joined, "mp", k) for k in range(1, parts)]
    order = jnp.concatenate(
        [(mine - jnp.arange(parts, dtype=jnp.int32)) % parts, across[None]]
    ).astype(jnp.int32)
    own, *sends = project(order, turns, weights)
    context = attend(
        session_length, own, [turn(part, "x", k) for k, part in enumerate(sends, 1)]
    )
    return (context, text_grad, image_grad)


def solution(mesh):
    fine = Mesh(mesh.devices.reshape(-1, XS, CS, mesh.shape["mp"]), (*DP, "mp"))
    return jax.shard_map(
        local,
        mesh=fine,
        in_specs=(
            P(DP),
            P(DP, None),
            P(DP),
            P(DP, "mp"),
            P(DP, "mp"),
            P(DP),
            P("mp"),
            P("mp"),
            P(DP, "mp"),
            P(DP, "mp"),
            P(DP, "mp"),
            P(DP, "mp"),
        ),
        out_specs=(P(DP, "mp"), P(DP, "mp"), P(DP, "mp")),
        check_vma=False,
    )
```

```python
import math

import jax
import jax.numpy as jnp
from jax import lax
from jax.experimental import pallas as pl
from jax.experimental.pallas import tpu as pltpu
from jax.sharding import Mesh
from jax.sharding import PartitionSpec as P

HD = 128
GAIN_ROWS = 8
VMEM_BYTES = 24 * 1024 * 1024
XS = 4
CS = 2
DP = ("z", "x", "c")


def pick(selector, values):
    return jnp.dot(selector, values, preferred_element_type=jnp.float32)


def iota(shape, axis):
    return lax.broadcasted_iota(jnp.int32, shape, axis)


def turned(row):
    count = row.shape[1]
    diagonal = iota((count, count), 0) == iota((count, count), 1)
    return jnp.sum(jnp.where(diagonal, row.astype(jnp.float32), 0.0), axis=1, keepdims=True)


def request_kernel(owner_ref, row_ref, requests_ref, codes_ref):
    count = owner_ref.shape[1]
    owner_row = owner_ref[...]
    owner_column = turned(owner_row).astype(jnp.int32)
    first, second = iota((count, count), 0), iota((count, count), 1)
    same = owner_row == owner_column
    earlier_column = jnp.sum(
        jnp.where(same & (second < first), 1.0, 0.0), axis=1, keepdims=True
    ).astype(jnp.int32)
    earlier_row = jnp.sum(
        jnp.where(same & (first < second), 1.0, 0.0), axis=0, keepdims=True
    ).astype(jnp.int32)
    asked = jnp.where(earlier_column == second, turned(row_ref[...]) + 1.0, 0.0)
    named = jnp.where(owner_row == first, 1.0, 0.0)
    found = pick(named.astype(jnp.bfloat16), asked.astype(jnp.bfloat16))
    requests_ref[...] = found.astype(jnp.int32) - 1
    codes_ref[...] = owner_row * (2 * XS) + earlier_row


def request(event_owner, event_row):
    count = event_row.shape[0]
    return pl.pallas_call(
        request_kernel,
        out_shape=[
            jax.ShapeDtypeStruct((count, HD), jnp.int32),
            jax.ShapeDtypeStruct((1, count), jnp.int32),
        ],
        compiler_params=pltpu.CompilerParams(vmem_limit_bytes=VMEM_BYTES),
        name="request",
    )(event_owner.reshape(1, count), event_row.reshape(1, count))


def join_kernel(text_ref, image_ref, price_ref, dir_ref, out_ref):
    columns = text_ref.shape[1]
    joined = (
        text_ref[...].astype(jnp.float32) * image_ref[...].astype(jnp.float32)
        + turned(price_ref[...]) * dir_ref[...].astype(jnp.float32)
    )
    width, depth = columns // XS, columns // XS // XS
    for x in range(XS):
        out_ref[:, x * width : (x + 1) * width] = jnp.concatenate(
            [joined[:, z * width + x * depth : z * width + (x + 1) * depth] for z in range(XS)],
            axis=1,
        ).astype(jnp.bfloat16)


def join(text_rows, image_rows, price, price_dir):
    return pl.pallas_call(
        join_kernel,
        out_shape=jax.ShapeDtypeStruct(text_rows.shape, jnp.bfloat16),
        compiler_params=pltpu.CompilerParams(vmem_limit_bytes=VMEM_BYTES),
        name="join",
    )(text_rows, image_rows, price.reshape(1, -1), price_dir.reshape(1, -1))


def answer_kernel(ids_ref, table_ref, out_ref):
    peers, table_rows = ids_ref.shape[0], table_ref.shape[0]
    count = 2 * peers
    width = table_ref.shape[1] // XS
    group = 2 * XS * CS
    target = iota((count, peers), 0)
    at = lax.rem(target, group)
    peer = (target - at) // 2 + lax.rem(at // 2, XS) * CS + at // (2 * XS)
    moved = jnp.where(peer == iota((count, peers), 1), 1.0, 0.0).astype(jnp.bfloat16)
    both = pick(moved, ids_ref[...].astype(jnp.float32).astype(jnp.bfloat16))
    lane, turn_of = iota(both.shape, 1), lax.rem(iota(both.shape, 0), 2)
    ids = jnp.sum(jnp.where(lane == turn_of, both, 0.0), axis=1, keepdims=True).astype(jnp.int32)
    wanted = jnp.where(ids == iota((count, table_rows), 1), 1.0, 0.0).astype(jnp.bfloat16)
    for block in range(XS):
        rows = pick(wanted, table_ref[:, block * width : (block + 1) * width]).astype(
            jnp.bfloat16
        )
        for z in range(count // group):
            to = (z * XS + block) * group
            out_ref[to : to + group, :] = rows[z * group : (z + 1) * group, :]


def answer(ids, table):
    return pl.pallas_call(
        answer_kernel,
        out_shape=jax.ShapeDtypeStruct(
            (2 * ids.shape[0] * XS, table.shape[1] // XS), jnp.bfloat16
        ),
        compiler_params=pltpu.CompilerParams(vmem_limit_bytes=VMEM_BYTES),
        name="answer",
    )(ids, table)


def select_kernel(codes_ref, replies_ref, gain_ref, out_ref):
    tokens, rows = codes_ref.shape[1], replies_ref.shape[0]
    replies = replies_ref[...]
    for x in range(XS):
        code = turned(codes_ref[x : x + 1, :]).astype(jnp.int32) + 2 * x
        chosen = jnp.where(code == iota((tokens, rows), 1), 1.0, 0.0).astype(jnp.bfloat16)
        out_ref[x * tokens : (x + 1) * tokens, :] = pick(chosen, replies).astype(jnp.bfloat16)
    out_ref[XS * tokens :, :] = jnp.broadcast_to(gain_ref[...], (GAIN_ROWS, gain_ref.shape[1]))


def select(codes, replies, gain):
    tokens, width = codes.size, replies.shape[1]
    return pl.pallas_call(
        select_kernel,
        out_shape=jax.ShapeDtypeStruct((tokens + GAIN_ROWS, width), jnp.bfloat16),
        compiler_params=pltpu.CompilerParams(vmem_limit_bytes=VMEM_BYTES),
        name="select",
    )(codes, replies, gain)


def project_kernel(
    order_ref, f0, f1, f2, f3, w_ref, own_ref, s1, s2, s3, acc_ref, normed_ref, held_ref, sum_ref, sem
):
    tokens = acc_ref.shape[0] // XS
    columns = acc_ref.shape[1]
    width = f0.shape[1]
    parts = (f0, f1, f2, f3)
    copies = []
    for k in range(len(parts)):
        there = pl.ds(pl.multiple_of(order_ref[k] * width, width), width)
        copies.append(
            pltpu.make_async_copy(
                w_ref.at[there, :], held_ref.at[k * width : (k + 1) * width, :], sem.at[k]
            )
        )
        copies[-1].start()

    total = jnp.zeros((XS * tokens, 1), jnp.float32)
    for k, part in enumerate(parts):
        value = part[: XS * tokens, :].astype(jnp.float32)
        gain = part[XS * tokens : XS * tokens + 1, :].astype(jnp.float32)
        total = total + jnp.sum(value * value, axis=1, keepdims=True)
        normed_ref[:, k * width : (k + 1) * width] = (value * gain).astype(jnp.bfloat16)
    sum_ref[...] = jnp.broadcast_to(total, sum_ref.shape)

    for copy in copies:
        copy.wait()
    tile = columns // 6
    for at in range(0, columns, tile):
        acc_ref[:, at : at + tile] = pick(normed_ref[...], held_ref[:, at : at + tile])

    mine = order_ref[XS]
    lane = iota((tokens, HD), 1)
    here = pl.ds(pl.multiple_of(mine * tokens, tokens), tokens)
    own_ref[:, :columns] = acc_ref[here, :]
    own_ref[:, columns:] = sum_ref[here, :]
    for k, out_ref in ((1, s1), (2, s2), (3, s3)):
        there = pl.ds(pl.multiple_of(lax.rem(mine + k, XS) * tokens, tokens), tokens)
        out_ref[:, :columns] = acc_ref[there, :].astype(jnp.bfloat16)
        total = sum_ref[there, :]
        high = total.astype(jnp.bfloat16).astype(jnp.float32)
        middle = (total - high).astype(jnp.bfloat16).astype(jnp.float32)
        low = total - high - middle
        out_ref[:, columns:] = jnp.where(
            lane == 0, high, jnp.where(lane == 1, middle, low)
        ).astype(jnp.bfloat16)


def project(order, turns, weights):
    rows, width = turns[0].shape
    tokens = (rows - GAIN_ROWS) // XS
    columns = weights.shape[1]
    vmem = pl.BlockSpec(memory_space=pltpu.VMEM)
    return pl.pallas_call(
        project_kernel,
        out_shape=[jax.ShapeDtypeStruct((tokens, columns + HD), jnp.float32)]
        + [jax.ShapeDtypeStruct((tokens, columns + HD), jnp.bfloat16)] * 3,
        in_specs=[pl.BlockSpec(memory_space=pltpu.SMEM)]
        + [vmem] * 4
        + [pl.BlockSpec(memory_space=pltpu.HBM)],
        out_specs=[vmem] * 4,
        scratch_shapes=[
            pltpu.VMEM((XS * tokens, columns), jnp.float32),
            pltpu.VMEM((XS * tokens, len(turns) * width), jnp.bfloat16),
            pltpu.VMEM(weights.shape, jnp.bfloat16),
            pltpu.VMEM((XS * tokens, HD), jnp.float32),
            pltpu.SemaphoreType.DMA((len(turns),)),
        ],
        compiler_params=pltpu.CompilerParams(vmem_limit_bytes=VMEM_BYTES),
        name="project",
    )(order, *turns, pltpu.with_memory_space_constraint(weights, pltpu.HBM))


def attend_kernel(length_ref, own_ref, p1, p2, p3, out_ref):
    tokens, width = out_ref.shape
    columns = 3 * width
    total = own_ref[:, columns : columns + 1]
    for part in (p1, p2, p3):
        pieces = part[:, columns : columns + HD].astype(jnp.float32)
        total = total + ((pieces[:, 0:1] + pieces[:, 1:2]) + pieces[:, 2:3])
    scale = lax.rsqrt(total / (8 * width) + 1e-06)
    length = length_ref[0]
    row = iota((tokens, tokens), 0)
    column = iota((tokens, tokens), 1)
    allowed = (column <= row) & (column < length)
    live = iota((tokens, HD), 0) < length
    for at in range(0, width, HD):
        query, keys, values = (
            (
                (
                    own_ref[:, a : a + HD]
                    + p1[:, a : a + HD].astype(jnp.float32)
                    + p2[:, a : a + HD].astype(jnp.float32)
                    + p3[:, a : a + HD].astype(jnp.float32)
                )
                * scale
            ).astype(jnp.bfloat16)
            for a in (at, width + at, 2 * width + at)
        )
        scores = lax.dot_general(
            query, keys, (((1,), (1,)), ((), ())), preferred_element_type=jnp.float32
        ) / math.sqrt(HD)
        scores = jnp.where(allowed, scores, jnp.float32(-1e30))
        powers = jnp.exp(scores - jnp.max(scores, axis=-1, keepdims=True))
        probs = (powers / jnp.sum(powers, axis=-1, keepdims=True)).astype(jnp.bfloat16)
        context = pick(probs, values)
        out_ref[:, at : at + HD] = jnp.where(live, context, 0.0).astype(jnp.bfloat16)


def attend(session_length, own, parts):
    tokens, columns = own.shape
    vmem = pl.BlockSpec(memory_space=pltpu.VMEM)
    return pl.pallas_call(
        attend_kernel,
        out_shape=jax.ShapeDtypeStruct((tokens, (columns - HD) // 3), jnp.bfloat16),
        in_specs=[pl.BlockSpec(memory_space=pltpu.SMEM)] + [vmem] * 4,
        out_specs=vmem,
        compiler_params=pltpu.CompilerParams(vmem_limit_bytes=VMEM_BYTES),
        name="attend",
    )(session_length, own, *parts)


def turn(value, axis, k):
    size = lax.axis_size(axis)
    return lax.ppermute(value, axis, [(i, (i + k) % size) for i in range(size)])


def exchange(value):
    return lax.all_to_all(value, DP, split_axis=0, concat_axis=0, tiled=True)


def local(
    session_length,
    event_owner,
    event_row,
    text_rows,
    image_rows,
    price,
    price_dir,
    norm_gain,
    w_query,
    w_key,
    w_value,
    cotangent,
):
    peers = lax.axis_size(DP)
    parts = lax.axis_size("mp")
    mine, across = lax.axis_index("mp"), lax.axis_index("x")
    tok_count = event_row.shape[0]
    capacity = 2 * tok_count // peers
    table_rows, col_width = text_rows.shape
    block = CS * w_query.shape[0]

    requests, codes = request(event_owner, event_row)
    got_ids = exchange(requests)
    w_query, w_key, w_value, _ = lax.optimization_barrier((w_query, w_key, w_value, requests))
    weights = lax.all_gather(
        jnp.concatenate([w_query, w_key, w_value], axis=1), ("z", "c"), axis=0, tiled=True
    )
    gain = lax.dynamic_index_in_dim(
        norm_gain.reshape(-1, XS, block), across, 1, keepdims=False
    ).reshape(1, -1)
    table = join(text_rows, image_rows, price, price_dir)
    all_codes = lax.all_gather(codes, "x", axis=0, tiled=True)
    got_ids, table, all_codes, gain = lax.optimization_barrier((got_ids, table, all_codes, gain))
    replies = exchange(
        answer(got_ids, table).reshape(peers, XS * capacity, col_width // XS)
    ).reshape(peers * XS * capacity, col_width // XS)

    slot_ids = codes[0] // (XS * capacity) * capacity + codes[0] % (XS * capacity)
    taken = jnp.arange(peers * capacity, dtype=jnp.int32)[:, None] == slot_ids[None, :]
    grad_buffer = (
        pick(taken.astype(jnp.bfloat16), cotangent)
        .astype(jnp.bfloat16)
        .reshape(peers, capacity, col_width)
    )
    grad_buffer, replies = lax.optimization_barrier((grad_buffer, replies))
    joined = select(all_codes, replies, gain)
    turns = [joined] + [turn(joined, "mp", k) for k in range(1, parts)]
    got_grads = exchange(grad_buffer).reshape(peers * capacity, col_width)
    ids = got_ids[:, :capacity].reshape(-1)
    wanted = (jnp.arange(table_rows, dtype=jnp.int32)[:, None] == ids[None, :]).astype(
        jnp.bfloat16
    )
    row_sums = pick(wanted, got_grads)
    text_grad = row_sums * image_rows.astype(jnp.float32)
    image_grad = row_sums * text_rows.astype(jnp.float32)

    order = jnp.concatenate(
        [(mine - jnp.arange(parts, dtype=jnp.int32)) % parts, across[None]]
    ).astype(jnp.int32)
    own, *sends = project(order, turns, weights)
    context = attend(
        session_length, own, [turn(part, "x", k) for k, part in enumerate(sends, 1)]
    )
    return (context, text_grad, image_grad)


def solution(mesh):
    fine = Mesh(mesh.devices.reshape(-1, XS, CS, mesh.shape["mp"]), (*DP, "mp"))
    return jax.shard_map(
        local,
        mesh=fine,
        in_specs=(
            P(DP),
            P(DP, None),
            P(DP),
            P(DP, "mp"),
            P(DP, "mp"),
            P(DP),
            P("mp"),
            P("mp"),
            P(DP, "mp"),
            P(DP, "mp"),
            P(DP, "mp"),
            P(DP, "mp"),
        ),
        out_specs=(P(DP, "mp"), P(DP, "mp"), P(DP, "mp")),
        check_vma=False,
    )
```

```python
import math

import jax
import jax.numpy as jnp
from jax import lax
from jax.experimental import pallas as pl
from jax.experimental.pallas import tpu as pltpu
from jax.sharding import Mesh
from jax.sharding import PartitionSpec as P

HD = 128
GAIN_ROWS = 8
VMEM_BYTES = 24 * 1024 * 1024
XS = 4
CS = 2
DP = ("z", "x", "c")


def pick(selector, values):
    return jnp.dot(selector, values, preferred_element_type=jnp.float32)


def iota(shape, axis):
    return lax.broadcasted_iota(jnp.int32, shape, axis)


def turned(row):
    count = row.shape[1]
    diagonal = iota((count, count), 0) == iota((count, count), 1)
    return jnp.sum(jnp.where(diagonal, row.astype(jnp.float32), 0.0), axis=1, keepdims=True)


def request_kernel(owner_ref, row_ref, wq_ref, wk_ref, wv_ref, requests_ref, codes_ref, w_ref):
    count = owner_ref.shape[1]
    owner_row = owner_ref[...]
    owner_column = turned(owner_row).astype(jnp.int32)
    first, second = iota((count, count), 0), iota((count, count), 1)
    same = owner_row == owner_column
    earlier_column = jnp.sum(
        jnp.where(same & (second < first), 1.0, 0.0), axis=1, keepdims=True
    ).astype(jnp.int32)
    earlier_row = jnp.sum(
        jnp.where(same & (first < second), 1.0, 0.0), axis=0, keepdims=True
    ).astype(jnp.int32)
    asked = jnp.where(earlier_column == second, turned(row_ref[...]) + 1.0, 0.0)
    named = jnp.where(owner_row == first, 1.0, 0.0)
    found = pick(named.astype(jnp.bfloat16), asked.astype(jnp.bfloat16))
    requests_ref[...] = found.astype(jnp.int32) - 1
    codes_ref[...] = owner_row * (2 * XS) + earlier_row
    width = wq_ref.shape[1]
    for k, part in enumerate((wq_ref, wk_ref, wv_ref)):
        w_ref[:, k * width : (k + 1) * width] = part[...]


def request(event_owner, event_row, *projections):
    count = event_row.shape[0]
    depth, width = projections[0].shape
    return pl.pallas_call(
        request_kernel,
        out_shape=[
            jax.ShapeDtypeStruct((count, HD), jnp.int32),
            jax.ShapeDtypeStruct((1, count), jnp.int32),
            jax.ShapeDtypeStruct((depth, 3 * width), jnp.bfloat16),
        ],
        name="request",
    )(event_owner.reshape(1, count), event_row.reshape(1, count), *projections)


def join_kernel(text_ref, image_ref, price_ref, dir_ref, out_ref):
    columns = text_ref.shape[1]
    joined = (
        text_ref[...].astype(jnp.float32) * image_ref[...].astype(jnp.float32)
        + turned(price_ref[...]) * dir_ref[...].astype(jnp.float32)
    )
    width, depth = columns // XS, columns // XS // XS
    for x in range(XS):
        out_ref[:, x * width : (x + 1) * width] = jnp.concatenate(
            [joined[:, z * width + x * depth : z * width + (x + 1) * depth] for z in range(XS)],
            axis=1,
        ).astype(jnp.bfloat16)


def join(text_rows, image_rows, price, price_dir):
    return pl.pallas_call(
        join_kernel,
        out_shape=jax.ShapeDtypeStruct(text_rows.shape, jnp.bfloat16),
        compiler_params=pltpu.CompilerParams(vmem_limit_bytes=VMEM_BYTES),
        name="join",
    )(text_rows, image_rows, price.reshape(1, -1), price_dir.reshape(1, -1))


def answer_kernel(ids_ref, table_ref, out_ref):
    peers, table_rows = ids_ref.shape[0], table_ref.shape[0]
    count = 2 * peers
    width = table_ref.shape[1] // XS
    group = 2 * XS * CS
    target = iota((count, peers), 0)
    at = lax.rem(target, group)
    peer = (target - at) // 2 + lax.rem(at // 2, XS) * CS + at // (2 * XS)
    moved = jnp.where(peer == iota((count, peers), 1), 1.0, 0.0).astype(jnp.bfloat16)
    both = pick(moved, ids_ref[...].astype(jnp.float32).astype(jnp.bfloat16))
    lane, turn_of = iota(both.shape, 1), lax.rem(iota(both.shape, 0), 2)
    ids = jnp.sum(jnp.where(lane == turn_of, both, 0.0), axis=1, keepdims=True).astype(jnp.int32)
    wanted = jnp.where(ids == iota((count, table_rows), 1), 1.0, 0.0).astype(jnp.bfloat16)
    for block in range(XS):
        rows = pick(wanted, table_ref[:, block * width : (block + 1) * width]).astype(
            jnp.bfloat16
        )
        for z in range(count // group):
            to = (z * XS + block) * group
            out_ref[to : to + group, :] = rows[z * group : (z + 1) * group, :]


def answer(ids, table):
    return pl.pallas_call(
        answer_kernel,
        out_shape=jax.ShapeDtypeStruct(
            (2 * ids.shape[0] * XS, table.shape[1] // XS), jnp.bfloat16
        ),
        compiler_params=pltpu.CompilerParams(vmem_limit_bytes=VMEM_BYTES),
        name="answer",
    )(ids, table)


def select_kernel(codes_ref, replies_ref, gain_ref, out_ref):
    tokens, rows = codes_ref.shape[1], replies_ref.shape[0]
    replies = replies_ref[...]
    for x in range(XS):
        code = turned(codes_ref[x : x + 1, :]).astype(jnp.int32) + 2 * x
        chosen = jnp.where(code == iota((tokens, rows), 1), 1.0, 0.0).astype(jnp.bfloat16)
        out_ref[x * tokens : (x + 1) * tokens, :] = pick(chosen, replies).astype(jnp.bfloat16)
    out_ref[XS * tokens :, :] = jnp.broadcast_to(gain_ref[...], (GAIN_ROWS, gain_ref.shape[1]))


def select(codes, replies, gain):
    tokens, width = codes.size, replies.shape[1]
    return pl.pallas_call(
        select_kernel,
        out_shape=jax.ShapeDtypeStruct((tokens + GAIN_ROWS, width), jnp.bfloat16),
        compiler_params=pltpu.CompilerParams(vmem_limit_bytes=VMEM_BYTES),
        name="select",
    )(codes, replies, gain)


def pack_kernel(codes_ref, grads_ref, out_ref):
    rows, width = out_ref.shape
    tokens = codes_ref.shape[1]
    number = iota((rows, tokens), 0)
    code = number // (2 * XS) * (2 * XS) + lax.rem(number, 2 * XS) // XS
    block = lax.rem(number, XS)
    total = jnp.zeros((rows, width), jnp.float32)
    for q in range(XS):
        chosen = jnp.where((codes_ref[...] == code) & (block == q), 1.0, 0.0).astype(jnp.bfloat16)
        total = total + pick(chosen, grads_ref[:, q * width : (q + 1) * width])
    out_ref[...] = total.astype(jnp.bfloat16)


def pack(codes, grads):
    rows, width = 2 * XS * grads.shape[0], grads.shape[1] // XS
    return pl.pallas_call(
        pack_kernel,
        out_shape=jax.ShapeDtypeStruct((rows, width), jnp.bfloat16),
        compiler_params=pltpu.CompilerParams(vmem_limit_bytes=VMEM_BYTES),
        cost_estimate=pl.CostEstimate(
            flops=16 * rows * grads.size, bytes_accessed=2 * rows * width, transcendentals=0
        ),
        name="pack",
    )(codes, grads)


def credit_kernel(ids_ref, grads_ref, text_ref, image_ref, text_out, image_out):
    peers, table_rows = ids_ref.shape[0], text_ref.shape[0]
    rows, width = grads_ref.shape
    spread = jnp.where(
        iota((peers, rows), 0) == iota((peers, rows), 1) // (2 * XS), 1.0, 0.0
    ).astype(jnp.bfloat16)
    both = lax.dot_general(
        ids_ref[...].astype(jnp.float32).astype(jnp.bfloat16),
        spread,
        (((0,), (0,)), ((), ())),
        preferred_element_type=jnp.float32,
    )
    turn_of = lax.rem(iota(both.shape, 1), 2 * XS) // XS
    ids = jnp.sum(jnp.where(iota(both.shape, 0) == turn_of, both, 0.0), axis=0, keepdims=True)
    number = iota((table_rows, rows), 1)
    named = iota((table_rows, rows), 0) == ids.astype(jnp.int32)
    for q in range(XS):
        at = slice(q * width, (q + 1) * width)
        chosen = jnp.where(named & (lax.rem(number, XS) == q), 1.0, 0.0).astype(jnp.bfloat16)
        total = pick(chosen, grads_ref[...])
        text_out[:, at] = total * image_ref[:, at].astype(jnp.float32)
        image_out[:, at] = total * text_ref[:, at].astype(jnp.float32)


def credit(ids, grads, text_rows, image_rows):
    out = jax.ShapeDtypeStruct(text_rows.shape, jnp.float32)
    return pl.pallas_call(
        credit_kernel,
        out_shape=[out, out],
        compiler_params=pltpu.CompilerParams(vmem_limit_bytes=VMEM_BYTES),
        name="credit",
    )(ids, grads, text_rows, image_rows)


def project_kernel(
    order_ref, f0, f1, f2, f3, w_ref, own_ref, s1, s2, s3, acc_ref, normed_ref, held_ref, sum_ref, sem
):
    tokens = acc_ref.shape[0] // XS
    columns = acc_ref.shape[1]
    width = f0.shape[1]
    parts = (f0, f1, f2, f3)
    copies = []
    for k in range(len(parts)):
        there = pl.ds(pl.multiple_of(order_ref[k] * width, width), width)
        copies.append(
            pltpu.make_async_copy(
                w_ref.at[there, :], held_ref.at[k * width : (k + 1) * width, :], sem.at[k]
            )
        )
        copies[-1].start()

    total = jnp.zeros((XS * tokens, 1), jnp.float32)
    for k, part in enumerate(parts):
        value = part[: XS * tokens, :].astype(jnp.float32)
        gain = part[XS * tokens : XS * tokens + 1, :].astype(jnp.float32)
        total = total + jnp.sum(value * value, axis=1, keepdims=True)
        normed_ref[:, k * width : (k + 1) * width] = (value * gain).astype(jnp.bfloat16)
    sum_ref[...] = jnp.broadcast_to(total, sum_ref.shape)

    for copy in copies:
        copy.wait()
    tile = columns // 6
    for at in range(0, columns, tile):
        acc_ref[:, at : at + tile] = pick(normed_ref[...], held_ref[:, at : at + tile])

    mine = order_ref[XS]
    lane = iota((tokens, HD), 1)
    here = pl.ds(pl.multiple_of(mine * tokens, tokens), tokens)
    own_ref[:, :columns] = acc_ref[here, :]
    own_ref[:, columns:] = sum_ref[here, :]
    for k, out_ref in ((1, s1), (2, s2), (3, s3)):
        there = pl.ds(pl.multiple_of(lax.rem(mine + k, XS) * tokens, tokens), tokens)
        out_ref[:, :columns] = acc_ref[there, :].astype(jnp.bfloat16)
        total = sum_ref[there, :]
        high = total.astype(jnp.bfloat16).astype(jnp.float32)
        middle = (total - high).astype(jnp.bfloat16).astype(jnp.float32)
        low = total - high - middle
        out_ref[:, columns:] = jnp.where(
            lane == 0, high, jnp.where(lane == 1, middle, low)
        ).astype(jnp.bfloat16)


def project(order, turns, weights):
    rows, width = turns[0].shape
    tokens = (rows - GAIN_ROWS) // XS
    columns = weights.shape[1]
    vmem = pl.BlockSpec(memory_space=pltpu.VMEM)
    return pl.pallas_call(
        project_kernel,
        out_shape=[jax.ShapeDtypeStruct((tokens, columns + HD), jnp.float32)]
        + [jax.ShapeDtypeStruct((tokens, columns + HD), jnp.bfloat16)] * 3,
        in_specs=[pl.BlockSpec(memory_space=pltpu.SMEM)]
        + [vmem] * 4
        + [pl.BlockSpec(memory_space=pltpu.HBM)],
        out_specs=[vmem] * 4,
        scratch_shapes=[
            pltpu.VMEM((XS * tokens, columns), jnp.float32),
            pltpu.VMEM((XS * tokens, len(turns) * width), jnp.bfloat16),
            pltpu.VMEM(weights.shape, jnp.bfloat16),
            pltpu.VMEM((XS * tokens, HD), jnp.float32),
            pltpu.SemaphoreType.DMA((len(turns),)),
        ],
        compiler_params=pltpu.CompilerParams(vmem_limit_bytes=VMEM_BYTES),
        cost_estimate=pl.CostEstimate(
            flops=64 * XS * tokens * weights.size, bytes_accessed=2 * weights.size, transcendentals=0
        ),
        name="project",
    )(order, *turns, pltpu.with_memory_space_constraint(weights, pltpu.HBM))


def attend_kernel(length_ref, own_ref, p1, p2, p3, out_ref):
    tokens, width = out_ref.shape
    columns = 3 * width
    total = own_ref[:, columns : columns + 1]
    for part in (p1, p2, p3):
        pieces = part[:, columns : columns + HD].astype(jnp.float32)
        total = total + ((pieces[:, 0:1] + pieces[:, 1:2]) + pieces[:, 2:3])
    scale = lax.rsqrt(total / (8 * width) + 1e-06)
    length = length_ref[0]
    row = iota((tokens, tokens), 0)
    column = iota((tokens, tokens), 1)
    allowed = (column <= row) & (column < length)
    live = iota((tokens, HD), 0) < length
    for at in range(0, width, HD):
        query, keys, values = (
            (
                (
                    own_ref[:, a : a + HD]
                    + p1[:, a : a + HD].astype(jnp.float32)
                    + p2[:, a : a + HD].astype(jnp.float32)
                    + p3[:, a : a + HD].astype(jnp.float32)
                )
                * scale
            ).astype(jnp.bfloat16)
            for a in (at, width + at, 2 * width + at)
        )
        scores = lax.dot_general(
            query, keys, (((1,), (1,)), ((), ())), preferred_element_type=jnp.float32
        ) / math.sqrt(HD)
        scores = jnp.where(allowed, scores, jnp.float32(-1e30))
        powers = jnp.exp(scores - jnp.max(scores, axis=-1, keepdims=True))
        probs = (powers / jnp.sum(powers, axis=-1, keepdims=True)).astype(jnp.bfloat16)
        context = pick(probs, values)
        out_ref[:, at : at + HD] = jnp.where(live, context, 0.0).astype(jnp.bfloat16)


def attend(session_length, own, parts):
    tokens, columns = own.shape
    vmem = pl.BlockSpec(memory_space=pltpu.VMEM)
    return pl.pallas_call(
        attend_kernel,
        out_shape=jax.ShapeDtypeStruct((tokens, (columns - HD) // 3), jnp.bfloat16),
        in_specs=[pl.BlockSpec(memory_space=pltpu.SMEM)] + [vmem] * 4,
        out_specs=vmem,
        compiler_params=pltpu.CompilerParams(vmem_limit_bytes=VMEM_BYTES),
        name="attend",
    )(session_length, own, *parts)


def turn(value, axis, k):
    size = lax.axis_size(axis)
    return lax.ppermute(value, axis, [(i, (i + k) % size) for i in range(size)])


def exchange(value):
    return lax.all_to_all(value, DP, split_axis=0, concat_axis=0, tiled=True)


def local(
    session_length,
    event_owner,
    event_row,
    text_rows,
    image_rows,
    price,
    price_dir,
    norm_gain,
    w_query,
    w_key,
    w_value,
    cotangent,
):
    peers = lax.axis_size(DP)
    parts = lax.axis_size("mp")
    mine, across = lax.axis_index("mp"), lax.axis_index("x")
    tok_count = event_row.shape[0]
    capacity = 2 * tok_count // peers
    col_width = text_rows.shape[1]
    block = CS * w_query.shape[0]

    requests, codes, joint = request(event_owner, event_row, w_query, w_key, w_value)
    got_ids = exchange(requests)
    weights = lax.all_gather(joint, ("z", "c"), axis=0, tiled=True)
    table = join(text_rows, image_rows, price, price_dir)
    got_ids, table = lax.optimization_barrier((got_ids, table))
    replies, codes, norm_gain = lax.optimization_barrier(
        (answer(got_ids, table), codes, norm_gain)
    )
    packed = (peers, XS * capacity, col_width // XS)
    flat = (peers * XS * capacity, col_width // XS)
    replies = exchange(replies.reshape(packed)).reshape(flat)
    gain = lax.dynamic_index_in_dim(
        norm_gain.reshape(-1, XS, block), across, 1, keepdims=False
    ).reshape(1, -1)
    all_codes = lax.all_gather(codes, "x", axis=0, tiled=True)
    order = jnp.concatenate(
        [(mine - jnp.arange(parts, dtype=jnp.int32)) % parts, across[None]]
    ).astype(jnp.int32)
    replies, all_codes, gain, order = lax.optimization_barrier((replies, all_codes, gain, order))
    joined = select(all_codes, replies, gain)
    turns = [joined] + [turn(joined, "mp", k) for k in range(1, parts)]
    codes, cotangent, _ = lax.optimization_barrier((codes, cotangent, joined))
    got_grads = exchange(pack(codes, cotangent).reshape(packed)).reshape(flat)

    own, *sends = project(order, turns, weights)
    far = turn(sends[1], "x", 2)
    context = attend(
        session_length, own, [turn(sends[0], "x", 1), far, turn(sends[2], "x", 3)]
    )
    context, got_grads = lax.optimization_barrier((context, got_grads))
    text_grad, image_grad = credit(got_ids, got_grads, text_rows, image_rows)
    return (context, text_grad, image_grad)


def solution(mesh):
    fine = Mesh(mesh.devices.reshape(-1, XS, CS, mesh.shape["mp"]), (*DP, "mp"))
    return jax.shard_map(
        local,
        mesh=fine,
        in_specs=(
            P(DP),
            P(DP, None),
            P(DP),
            P(DP, "mp"),
            P(DP, "mp"),
            P(DP),
            P("mp"),
            P("mp"),
            P(DP, "mp"),
            P(DP, "mp"),
            P(DP, "mp"),
            P(DP, "mp"),
        ),
        out_specs=(P(DP, "mp"), P(DP, "mp"), P(DP, "mp")),
        check_vma=False,
    )
```

```python
import functools
import math

import jax
import jax.numpy as jnp
from jax import lax
from jax.experimental import pallas as pl
from jax.experimental.pallas import tpu as pltpu
from jax.sharding import Mesh
from jax.sharding import PartitionSpec as P

HD = 128
GAIN_ROWS = 8
VMEM_BYTES = 24 * 1024 * 1024
XS = 4
CS = 2
DP = ("z", "x", "c")


def pick(selector, values):
    return jnp.dot(selector, values, preferred_element_type=jnp.float32)


def iota(shape, axis):
    return lax.broadcasted_iota(jnp.int32, shape, axis)


def turned(row):
    count = row.shape[1]
    diagonal = iota((count, count), 0) == iota((count, count), 1)
    return jnp.sum(jnp.where(diagonal, row.astype(jnp.float32), 0.0), axis=1, keepdims=True)


def request_kernel(owner_ref, row_ref, wq_ref, wk_ref, wv_ref, requests_ref, codes_ref, w_ref):
    count = owner_ref.shape[1]
    owner_row = owner_ref[...]
    owner_column = turned(owner_row).astype(jnp.int32)
    first, second = iota((count, count), 0), iota((count, count), 1)
    same = owner_row == owner_column
    earlier_column = jnp.sum(
        jnp.where(same & (second < first), 1.0, 0.0), axis=1, keepdims=True
    ).astype(jnp.int32)
    earlier_row = jnp.sum(
        jnp.where(same & (first < second), 1.0, 0.0), axis=0, keepdims=True
    ).astype(jnp.int32)
    asked = jnp.where(earlier_column == second, turned(row_ref[...]) + 1.0, 0.0)
    named = jnp.where(owner_row == first, 1.0, 0.0)
    found = pick(named.astype(jnp.bfloat16), asked.astype(jnp.bfloat16))
    requests_ref[...] = found.astype(jnp.int32) - 1
    codes_ref[...] = owner_row * (2 * XS) + earlier_row
    width = wq_ref.shape[1]
    for k, part in enumerate((wq_ref, wk_ref, wv_ref)):
        w_ref[:, k * width : (k + 1) * width] = part[...]


def request(event_owner, event_row, *projections):
    count = event_row.shape[0]
    depth, width = projections[0].shape
    return pl.pallas_call(
        request_kernel,
        out_shape=[
            jax.ShapeDtypeStruct((count, HD), jnp.int32),
            jax.ShapeDtypeStruct((1, count), jnp.int32),
            jax.ShapeDtypeStruct((depth, 3 * width), jnp.bfloat16),
        ],
        name="request",
    )(event_owner.reshape(1, count), event_row.reshape(1, count), *projections)


def join_kernel(text_ref, image_ref, price_ref, dir_ref, out_ref):
    columns = text_ref.shape[1]
    joined = (
        text_ref[...].astype(jnp.float32) * image_ref[...].astype(jnp.float32)
        + turned(price_ref[...]) * dir_ref[...].astype(jnp.float32)
    )
    width, depth = columns // XS, columns // XS // XS
    for x in range(XS):
        out_ref[:, x * width : (x + 1) * width] = jnp.concatenate(
            [joined[:, z * width + x * depth : z * width + (x + 1) * depth] for z in range(XS)],
            axis=1,
        ).astype(jnp.bfloat16)


def join(text_rows, image_rows, price, price_dir):
    return pl.pallas_call(
        join_kernel,
        out_shape=jax.ShapeDtypeStruct(text_rows.shape, jnp.bfloat16),
        compiler_params=pltpu.CompilerParams(vmem_limit_bytes=VMEM_BYTES),
        name="join",
    )(text_rows, image_rows, price.reshape(1, -1), price_dir.reshape(1, -1))


def answer_kernel(ids_ref, table_ref, out_ref):
    peers, table_rows = ids_ref.shape[0], table_ref.shape[0]
    count = 2 * peers
    width = table_ref.shape[1] // XS
    group = 2 * XS * CS
    target = iota((count, peers), 0)
    at = lax.rem(target, group)
    peer = (target - at) // 2 + lax.rem(at // 2, XS) * CS + at // (2 * XS)
    moved = jnp.where(peer == iota((count, peers), 1), 1.0, 0.0).astype(jnp.bfloat16)
    both = pick(moved, ids_ref[...].astype(jnp.float32).astype(jnp.bfloat16))
    lane, turn_of = iota(both.shape, 1), lax.rem(iota(both.shape, 0), 2)
    ids = jnp.sum(jnp.where(lane == turn_of, both, 0.0), axis=1, keepdims=True).astype(jnp.int32)
    wanted = jnp.where(ids == iota((count, table_rows), 1), 1.0, 0.0).astype(jnp.bfloat16)
    for block in range(XS):
        rows = pick(wanted, table_ref[:, block * width : (block + 1) * width]).astype(
            jnp.bfloat16
        )
        for z in range(count // group):
            to = (z * XS + block) * group
            out_ref[to : to + group, :] = rows[z * group : (z + 1) * group, :]


def answer(ids, table):
    return pl.pallas_call(
        answer_kernel,
        out_shape=jax.ShapeDtypeStruct(
            (2 * ids.shape[0] * XS, table.shape[1] // XS), jnp.bfloat16
        ),
        compiler_params=pltpu.CompilerParams(vmem_limit_bytes=VMEM_BYTES),
        name="answer",
    )(ids, table)


def select_kernel(codes_ref, replies_ref, gain_ref, out_ref):
    tokens, rows = codes_ref.shape[1], replies_ref.shape[0]
    replies = replies_ref[...]
    for x in range(XS):
        code = turned(codes_ref[x : x + 1, :]).astype(jnp.int32) + 2 * x
        chosen = jnp.where(code == iota((tokens, rows), 1), 1.0, 0.0).astype(jnp.bfloat16)
        out_ref[x * tokens : (x + 1) * tokens, :] = pick(chosen, replies).astype(jnp.bfloat16)
    out_ref[XS * tokens :, :] = jnp.broadcast_to(gain_ref[...], (GAIN_ROWS, gain_ref.shape[1]))


def select(codes, replies, gain):
    tokens, width = codes.size, replies.shape[1]
    return pl.pallas_call(
        select_kernel,
        out_shape=jax.ShapeDtypeStruct((tokens + GAIN_ROWS, width), jnp.bfloat16),
        compiler_params=pltpu.CompilerParams(vmem_limit_bytes=VMEM_BYTES),
        name="select",
    )(codes, replies, gain)


def pack_kernel(codes_ref, grads_ref, out_ref):
    rows, width = out_ref.shape
    tokens = codes_ref.shape[1]
    number = iota((rows, tokens), 0)
    code = number // (2 * XS) * (2 * XS) + lax.rem(number, 2 * XS) // XS
    block = lax.rem(number, XS)
    total = jnp.zeros((rows, width), jnp.float32)
    for q in range(XS):
        chosen = jnp.where((codes_ref[...] == code) & (block == q), 1.0, 0.0).astype(jnp.bfloat16)
        total = total + pick(chosen, grads_ref[:, q * width : (q + 1) * width])
    out_ref[...] = total.astype(jnp.bfloat16)


def pack(codes, grads):
    rows, width = 2 * XS * grads.shape[0], grads.shape[1] // XS
    return pl.pallas_call(
        pack_kernel,
        out_shape=jax.ShapeDtypeStruct((rows, width), jnp.bfloat16),
        compiler_params=pltpu.CompilerParams(vmem_limit_bytes=VMEM_BYTES),
        cost_estimate=pl.CostEstimate(
            flops=16 * rows * grads.size, bytes_accessed=2 * rows * width, transcendentals=0
        ),
        name="pack",
    )(codes, grads)


def credit_kernel(ids_ref, grads_ref, text_ref, image_ref, text_out, image_out):
    peers, table_rows = ids_ref.shape[0], text_ref.shape[0]
    rows, width = grads_ref.shape
    spread = jnp.where(
        iota((peers, rows), 0) == iota((peers, rows), 1) // (2 * XS), 1.0, 0.0
    ).astype(jnp.bfloat16)
    both = lax.dot_general(
        ids_ref[...].astype(jnp.float32).astype(jnp.bfloat16),
        spread,
        (((0,), (0,)), ((), ())),
        preferred_element_type=jnp.float32,
    )
    turn_of = lax.rem(iota(both.shape, 1), 2 * XS) // XS
    ids = jnp.sum(jnp.where(iota(both.shape, 0) == turn_of, both, 0.0), axis=0, keepdims=True)
    number = iota((table_rows, rows), 1)
    named = iota((table_rows, rows), 0) == ids.astype(jnp.int32)
    for q in range(XS):
        at = slice(q * width, (q + 1) * width)
        chosen = jnp.where(named & (lax.rem(number, XS) == q), 1.0, 0.0).astype(jnp.bfloat16)
        total = pick(chosen, grads_ref[...])
        text_out[:, at] = total * image_ref[:, at].astype(jnp.float32)
        image_out[:, at] = total * text_ref[:, at].astype(jnp.float32)


def credit(ids, grads, text_rows, image_rows):
    out = jax.ShapeDtypeStruct(text_rows.shape, jnp.float32)
    return pl.pallas_call(
        credit_kernel,
        out_shape=[out, out],
        compiler_params=pltpu.CompilerParams(vmem_limit_bytes=VMEM_BYTES),
        name="credit",
    )(ids, grads, text_rows, image_rows)


def project_kernel(shifts, order_ref, f0, f1, f2, f3, w_ref, *refs):
    outs, (acc_ref, normed_ref, held_ref, sum_ref, sem) = refs[: len(shifts)], refs[len(shifts) :]
    tokens = acc_ref.shape[0] // len(shifts)
    columns = acc_ref.shape[1]
    width = f0.shape[1]
    parts = (f0, f1, f2, f3)
    copies = []
    for k in range(len(parts)):
        there = pl.ds(pl.multiple_of(order_ref[k] * width, width), width)
        copies.append(
            pltpu.make_async_copy(
                w_ref.at[there, :], held_ref.at[k * width : (k + 1) * width, :], sem.at[k]
            )
        )
        copies[-1].start()

    mine = order_ref[XS]
    for n, shift in enumerate(shifts):
        rows = slice(n * tokens, (n + 1) * tokens)
        there = pl.ds(pl.multiple_of(lax.rem(mine + shift, XS) * tokens, tokens), tokens)
        total = jnp.zeros((tokens, 1), jnp.float32)
        for k, part in enumerate(parts):
            value = part[there, :].astype(jnp.float32)
            gain = part[XS * tokens : XS * tokens + 1, :].astype(jnp.float32)
            total = total + jnp.sum(value * value, axis=1, keepdims=True)
            normed_ref[rows, k * width : (k + 1) * width] = (value * gain).astype(jnp.bfloat16)
        sum_ref[rows, :] = jnp.broadcast_to(total, (tokens, HD))

    for copy in copies:
        copy.wait()
    tile = columns // 6
    for at in range(0, columns, tile):
        acc_ref[:, at : at + tile] = pick(normed_ref[...], held_ref[:, at : at + tile])

    lane = iota((tokens, HD), 1)
    for n, (shift, out_ref) in enumerate(zip(shifts, outs)):
        rows = slice(n * tokens, (n + 1) * tokens)
        total = sum_ref[rows, :]
        if shift == 0:
            out_ref[:, :columns] = acc_ref[rows, :]
            out_ref[:, columns:] = total
        else:
            out_ref[:, :columns] = acc_ref[rows, :].astype(jnp.bfloat16)
            high = total.astype(jnp.bfloat16).astype(jnp.float32)
            middle = (total - high).astype(jnp.bfloat16).astype(jnp.float32)
            low = total - high - middle
            out_ref[:, columns:] = jnp.where(
                lane == 0, high, jnp.where(lane == 1, middle, low)
            ).astype(jnp.bfloat16)


def project(shifts, order, turns, weights):
    rows, width = turns[0].shape
    tokens = (rows - GAIN_ROWS) // XS
    columns = weights.shape[1]
    vmem = pl.BlockSpec(memory_space=pltpu.VMEM)
    return pl.pallas_call(
        functools.partial(project_kernel, shifts),
        out_shape=[
            jax.ShapeDtypeStruct((tokens, columns + HD), jnp.bfloat16 if shift else jnp.float32)
            for shift in shifts
        ],
        in_specs=[pl.BlockSpec(memory_space=pltpu.SMEM)]
        + [vmem] * 4
        + [pl.BlockSpec(memory_space=pltpu.HBM)],
        out_specs=[vmem] * len(shifts),
        scratch_shapes=[
            pltpu.VMEM((len(shifts) * tokens, columns), jnp.float32),
            pltpu.VMEM((len(shifts) * tokens, len(turns) * width), jnp.bfloat16),
            pltpu.VMEM(weights.shape, jnp.bfloat16),
            pltpu.VMEM((len(shifts) * tokens, HD), jnp.float32),
            pltpu.SemaphoreType.DMA((len(turns),)),
        ],
        compiler_params=pltpu.CompilerParams(vmem_limit_bytes=VMEM_BYTES),
        cost_estimate=pl.CostEstimate(
            flops=64 * len(shifts) * tokens * weights.size,
            bytes_accessed=2 * weights.size,
            transcendentals=0,
        ),
        name="project",
    )(order, *turns, pltpu.with_memory_space_constraint(weights, pltpu.HBM))


def attend_kernel(length_ref, own_ref, p1, p2, p3, out_ref):
    tokens, width = out_ref.shape
    columns = 3 * width
    total = own_ref[:, columns : columns + 1]
    for part in (p1, p2, p3):
        pieces = part[:, columns : columns + HD].astype(jnp.float32)
        total = total + ((pieces[:, 0:1] + pieces[:, 1:2]) + pieces[:, 2:3])
    scale = lax.rsqrt(total / (8 * width) + 1e-06)
    length = length_ref[0]
    row = iota((tokens, tokens), 0)
    column = iota((tokens, tokens), 1)
    allowed = (column <= row) & (column < length)
    live = iota((tokens, HD), 0) < length
    for at in range(0, width, HD):
        query, keys, values = (
            (
                (
                    own_ref[:, a : a + HD]
                    + p1[:, a : a + HD].astype(jnp.float32)
                    + p2[:, a : a + HD].astype(jnp.float32)
                    + p3[:, a : a + HD].astype(jnp.float32)
                )
                * scale
            ).astype(jnp.bfloat16)
            for a in (at, width + at, 2 * width + at)
        )
        scores = lax.dot_general(
            query, keys, (((1,), (1,)), ((), ())), preferred_element_type=jnp.float32
        ) / math.sqrt(HD)
        scores = jnp.where(allowed, scores, jnp.float32(-1e30))
        powers = jnp.exp(scores - jnp.max(scores, axis=-1, keepdims=True))
        probs = (powers / jnp.sum(powers, axis=-1, keepdims=True)).astype(jnp.bfloat16)
        context = pick(probs, values)
        out_ref[:, at : at + HD] = jnp.where(live, context, 0.0).astype(jnp.bfloat16)


def attend(session_length, own, parts):
    tokens, columns = own.shape
    vmem = pl.BlockSpec(memory_space=pltpu.VMEM)
    return pl.pallas_call(
        attend_kernel,
        out_shape=jax.ShapeDtypeStruct((tokens, (columns - HD) // 3), jnp.bfloat16),
        in_specs=[pl.BlockSpec(memory_space=pltpu.SMEM)] + [vmem] * 4,
        out_specs=vmem,
        compiler_params=pltpu.CompilerParams(vmem_limit_bytes=VMEM_BYTES),
        name="attend",
    )(session_length, own, *parts)


def turn(value, axis, k):
    size = lax.axis_size(axis)
    return lax.ppermute(value, axis, [(i, (i + k) % size) for i in range(size)])


def exchange(value):
    return lax.all_to_all(value, DP, split_axis=0, concat_axis=0, tiled=True)


def local(
    session_length,
    event_owner,
    event_row,
    text_rows,
    image_rows,
    price,
    price_dir,
    norm_gain,
    w_query,
    w_key,
    w_value,
    cotangent,
):
    peers = lax.axis_size(DP)
    parts = lax.axis_size("mp")
    mine, across = lax.axis_index("mp"), lax.axis_index("x")
    tok_count = event_row.shape[0]
    capacity = 2 * tok_count // peers
    col_width = text_rows.shape[1]
    block = CS * w_query.shape[0]

    requests, codes, joint = request(event_owner, event_row, w_query, w_key, w_value)
    got_ids = exchange(requests)
    weights = lax.all_gather(joint, ("z", "c"), axis=0, tiled=True)
    table = join(text_rows, image_rows, price, price_dir)
    got_ids, table = lax.optimization_barrier((got_ids, table))
    replies, codes, norm_gain = lax.optimization_barrier(
        (answer(got_ids, table), codes, norm_gain)
    )
    packed = (peers, XS * capacity, col_width // XS)
    flat = (peers * XS * capacity, col_width // XS)
    replies = exchange(replies.reshape(packed)).reshape(flat)
    gain = lax.dynamic_index_in_dim(
        norm_gain.reshape(-1, XS, block), across, 1, keepdims=False
    ).reshape(1, -1)
    grads = pack(codes, cotangent)
    all_codes = lax.all_gather(codes, "x", axis=0, tiled=True)
    order = jnp.concatenate(
        [(mine - jnp.arange(parts, dtype=jnp.int32)) % parts, across[None]]
    ).astype(jnp.int32)
    replies, all_codes, gain, order, grads = lax.optimization_barrier(
        (replies, all_codes, gain, order, grads)
    )
    joined = select(all_codes, replies, gain)
    turns = [joined] + [turn(joined, "mp", k) for k in range(1, parts)]
    grads, _ = lax.optimization_barrier((grads, joined))
    got_grads = exchange(grads.reshape(packed)).reshape(flat)

    (far,) = project((2,), order, turns, weights)
    own, after, before = project((0, 1, 3), order, turns, weights)
    context = attend(
        session_length, own, [turn(after, "x", 1), turn(far, "x", 2), turn(before, "x", 3)]
    )
    context, got_grads = lax.optimization_barrier((context, got_grads))
    text_grad, image_grad = credit(got_ids, got_grads, text_rows, image_rows)
    return (context, text_grad, image_grad)


def solution(mesh):
    fine = Mesh(mesh.devices.reshape(-1, XS, CS, mesh.shape["mp"]), (*DP, "mp"))
    return jax.shard_map(
        local,
        mesh=fine,
        in_specs=(
            P(DP),
            P(DP, None),
            P(DP),
            P(DP, "mp"),
            P(DP, "mp"),
            P(DP),
            P("mp"),
            P("mp"),
            P(DP, "mp"),
            P(DP, "mp"),
            P(DP, "mp"),
            P(DP, "mp"),
        ),
        out_specs=(P(DP, "mp"), P(DP, "mp"), P(DP, "mp")),
        check_vma=False,
    )
```

```python
import functools
import math

import jax
import jax.numpy as jnp
from jax import lax
from jax.experimental import pallas as pl
from jax.experimental.pallas import tpu as pltpu
from jax.sharding import Mesh
from jax.sharding import PartitionSpec as P

HD = 128
GAIN_ROWS = 8
VMEM_BYTES = 24 * 1024 * 1024
XS = 4
CS = 2
DP = ("z", "x", "c")


def pick(selector, values):
    return jnp.dot(selector, values, preferred_element_type=jnp.float32)


def iota(shape, axis):
    return lax.broadcasted_iota(jnp.int32, shape, axis)


def turned(row):
    count = row.shape[1]
    diagonal = iota((count, count), 0) == iota((count, count), 1)
    return jnp.sum(jnp.where(diagonal, row.astype(jnp.float32), 0.0), axis=1, keepdims=True)


def request_kernel(owner_ref, row_ref, wq_ref, wk_ref, wv_ref, requests_ref, codes_ref, w_ref):
    count = owner_ref.shape[1]
    owner_row = owner_ref[...]
    owner_column = turned(owner_row).astype(jnp.int32)
    first, second = iota((count, count), 0), iota((count, count), 1)
    same = owner_row == owner_column
    earlier_column = jnp.sum(
        jnp.where(same & (second < first), 1.0, 0.0), axis=1, keepdims=True
    ).astype(jnp.int32)
    earlier_row = jnp.sum(
        jnp.where(same & (first < second), 1.0, 0.0), axis=0, keepdims=True
    ).astype(jnp.int32)
    asked = jnp.where(earlier_column == second, turned(row_ref[...]) + 1.0, 0.0)
    named = jnp.where(owner_row == first, 1.0, 0.0)
    found = pick(named.astype(jnp.bfloat16), asked.astype(jnp.bfloat16))
    requests_ref[...] = found.astype(jnp.int32) - 1
    codes_ref[...] = owner_row * (2 * XS) + earlier_row
    width = wq_ref.shape[1]
    for k, part in enumerate((wq_ref, wk_ref, wv_ref)):
        w_ref[:, k * width : (k + 1) * width] = part[...]


def request(event_owner, event_row, *projections):
    count = event_row.shape[0]
    depth, width = projections[0].shape
    return pl.pallas_call(
        request_kernel,
        out_shape=[
            jax.ShapeDtypeStruct((count, HD), jnp.int32),
            jax.ShapeDtypeStruct((1, count), jnp.int32),
            jax.ShapeDtypeStruct((depth, 3 * width), jnp.bfloat16),
        ],
        name="request",
    )(event_owner.reshape(1, count), event_row.reshape(1, count), *projections)


def join_kernel(text_ref, image_ref, price_ref, dir_ref, out_ref):
    columns = text_ref.shape[1]
    joined = (
        text_ref[...].astype(jnp.float32) * image_ref[...].astype(jnp.float32)
        + turned(price_ref[...]) * dir_ref[...].astype(jnp.float32)
    )
    width, depth = columns // XS, columns // XS // XS
    for x in range(XS):
        out_ref[:, x * width : (x + 1) * width] = jnp.concatenate(
            [joined[:, z * width + x * depth : z * width + (x + 1) * depth] for z in range(XS)],
            axis=1,
        ).astype(jnp.bfloat16)


def join(text_rows, image_rows, price, price_dir):
    return pl.pallas_call(
        join_kernel,
        out_shape=jax.ShapeDtypeStruct(text_rows.shape, jnp.bfloat16),
        compiler_params=pltpu.CompilerParams(vmem_limit_bytes=VMEM_BYTES),
        name="join",
    )(text_rows, image_rows, price.reshape(1, -1), price_dir.reshape(1, -1))


def answer_kernel(ids_ref, table_ref, out_ref):
    peers, table_rows = ids_ref.shape[0], table_ref.shape[0]
    count = 2 * peers
    width = table_ref.shape[1] // XS
    group = 2 * XS * CS
    target = iota((count, peers), 0)
    at = lax.rem(target, group)
    peer = (target - at) // 2 + lax.rem(at // 2, XS) * CS + at // (2 * XS)
    moved = jnp.where(peer == iota((count, peers), 1), 1.0, 0.0).astype(jnp.bfloat16)
    both = pick(moved, ids_ref[...].astype(jnp.float32).astype(jnp.bfloat16))
    lane, turn_of = iota(both.shape, 1), lax.rem(iota(both.shape, 0), 2)
    ids = jnp.sum(jnp.where(lane == turn_of, both, 0.0), axis=1, keepdims=True).astype(jnp.int32)
    wanted = jnp.where(ids == iota((count, table_rows), 1), 1.0, 0.0).astype(jnp.bfloat16)
    for block in range(XS):
        rows = pick(wanted, table_ref[:, block * width : (block + 1) * width]).astype(
            jnp.bfloat16
        )
        for z in range(count // group):
            to = (z * XS + block) * group
            out_ref[to : to + group, :] = rows[z * group : (z + 1) * group, :]


def answer(ids, table):
    return pl.pallas_call(
        answer_kernel,
        out_shape=jax.ShapeDtypeStruct(
            (2 * ids.shape[0] * XS, table.shape[1] // XS), jnp.bfloat16
        ),
        compiler_params=pltpu.CompilerParams(vmem_limit_bytes=VMEM_BYTES),
        name="answer",
    )(ids, table)


def select_kernel(codes_ref, replies_ref, gain_ref, out_ref):
    tokens, rows = codes_ref.shape[1], replies_ref.shape[0]
    replies = replies_ref[...]
    for x in range(XS):
        code = turned(codes_ref[x : x + 1, :]).astype(jnp.int32) + 2 * x
        chosen = jnp.where(code == iota((tokens, rows), 1), 1.0, 0.0).astype(jnp.bfloat16)
        out_ref[x * tokens : (x + 1) * tokens, :] = pick(chosen, replies).astype(jnp.bfloat16)
    out_ref[XS * tokens :, :] = jnp.broadcast_to(gain_ref[...], (GAIN_ROWS, gain_ref.shape[1]))


def select(codes, replies, gain):
    tokens, width = codes.size, replies.shape[1]
    return pl.pallas_call(
        select_kernel,
        out_shape=jax.ShapeDtypeStruct((tokens + GAIN_ROWS, width), jnp.bfloat16),
        compiler_params=pltpu.CompilerParams(vmem_limit_bytes=VMEM_BYTES),
        name="select",
    )(codes, replies, gain)


def pack_kernel(codes_ref, grads_ref, out_ref):
    rows, width = out_ref.shape
    tokens = codes_ref.shape[1]
    number = iota((rows, tokens), 0)
    code = number // (2 * XS) * (2 * XS) + lax.rem(number, 2 * XS) // XS
    block = lax.rem(number, XS)
    total = jnp.zeros((rows, width), jnp.float32)
    for q in range(XS):
        chosen = jnp.where((codes_ref[...] == code) & (block == q), 1.0, 0.0).astype(jnp.bfloat16)
        total = total + pick(chosen, grads_ref[:, q * width : (q + 1) * width])
    out_ref[...] = total.astype(jnp.bfloat16)


def pack(codes, grads):
    rows, width = 2 * XS * grads.shape[0], grads.shape[1] // XS
    return pl.pallas_call(
        pack_kernel,
        out_shape=jax.ShapeDtypeStruct((rows, width), jnp.bfloat16),
        compiler_params=pltpu.CompilerParams(vmem_limit_bytes=VMEM_BYTES),
        cost_estimate=pl.CostEstimate(
            flops=16 * rows * grads.size, bytes_accessed=2 * rows * width, transcendentals=0
        ),
        name="pack",
    )(codes, grads)


def credit_kernel(ids_ref, grads_ref, text_ref, image_ref, text_out, image_out):
    peers, table_rows = ids_ref.shape[0], text_ref.shape[0]
    rows, width = grads_ref.shape
    spread = jnp.where(
        iota((peers, rows), 0) == iota((peers, rows), 1) // (2 * XS), 1.0, 0.0
    ).astype(jnp.bfloat16)
    both = lax.dot_general(
        ids_ref[...].astype(jnp.float32).astype(jnp.bfloat16),
        spread,
        (((0,), (0,)), ((), ())),
        preferred_element_type=jnp.float32,
    )
    turn_of = lax.rem(iota(both.shape, 1), 2 * XS) // XS
    ids = jnp.sum(jnp.where(iota(both.shape, 0) == turn_of, both, 0.0), axis=0, keepdims=True)
    number = iota((table_rows, rows), 1)
    named = iota((table_rows, rows), 0) == ids.astype(jnp.int32)
    for q in range(XS):
        at = slice(q * width, (q + 1) * width)
        chosen = jnp.where(named & (lax.rem(number, XS) == q), 1.0, 0.0).astype(jnp.bfloat16)
        total = pick(chosen, grads_ref[...])
        text_out[:, at] = total * image_ref[:, at].astype(jnp.float32)
        image_out[:, at] = total * text_ref[:, at].astype(jnp.float32)


def credit(ids, grads, text_rows, image_rows):
    out = jax.ShapeDtypeStruct(text_rows.shape, jnp.float32)
    return pl.pallas_call(
        credit_kernel,
        out_shape=[out, out],
        compiler_params=pltpu.CompilerParams(vmem_limit_bytes=VMEM_BYTES),
        name="credit",
    )(ids, grads, text_rows, image_rows)


def project_kernel(shifts, order_ref, f0, f1, f2, f3, w_ref, *refs):
    outs, (acc_ref, normed_ref, held_ref, sum_ref, sem) = refs[: len(shifts)], refs[len(shifts) :]
    tokens = acc_ref.shape[0] // len(shifts)
    columns = acc_ref.shape[1]
    width = f0.shape[1]
    parts = (f0, f1, f2, f3)
    tile = columns // 6
    copies = []
    for n in range(columns // tile):
        at = slice(n * tile, (n + 1) * tile)
        copies.append(pltpu.make_async_copy(w_ref.at[:, at], held_ref.at[:, at], sem.at[n]))
        copies[-1].start()

    mine = order_ref[XS]
    for n, (shift, _) in enumerate(shifts):
        rows = slice(n * tokens, (n + 1) * tokens)
        there = pl.ds(pl.multiple_of(lax.rem(mine + shift, XS) * tokens, tokens), tokens)
        total = jnp.zeros((tokens, 1), jnp.float32)
        for k, part in enumerate(parts):
            value = part[there, :].astype(jnp.float32)
            gain = part[XS * tokens : XS * tokens + 1, :].astype(jnp.float32)
            total = total + jnp.sum(value * value, axis=1, keepdims=True)
            held = pl.ds(pl.multiple_of(order_ref[k] * width, width), width)
            normed_ref[rows, held] = (value * gain).astype(jnp.bfloat16)
        sum_ref[rows, :] = jnp.broadcast_to(total, (tokens, HD))

    for n, copy in enumerate(copies):
        copy.wait()
        at = slice(n * tile, (n + 1) * tile)
        acc_ref[:, at] = pick(normed_ref[...], held_ref[:, at])

    for n, ((_, wide), out_ref) in enumerate(zip(shifts, outs)):
        rows = slice(n * tokens, (n + 1) * tokens)
        out_ref[:, :columns] = acc_ref[rows, :].astype(out_ref.dtype)
        out_ref[:, columns:] = sum_ref[rows, :] if wide else pieces(sum_ref[rows, :])


def pieces(total):
    high = total.astype(jnp.bfloat16).astype(jnp.float32)
    middle = (total - high).astype(jnp.bfloat16).astype(jnp.float32)
    lane = iota(total.shape, 1)
    return jnp.where(lane == 0, high, jnp.where(lane == 1, middle, total - high - middle)).astype(
        jnp.bfloat16
    )


def whole(lanes):
    value = lanes.astype(jnp.float32)
    return (value[:, 0:1] + value[:, 1:2]) + value[:, 2:3]


def add_kernel(mine_ref, theirs_ref, out_ref):
    columns = out_ref.shape[1] - HD
    out_ref[:, :columns] = (
        mine_ref[:, :columns] + theirs_ref[:, :columns].astype(jnp.float32)
    ).astype(jnp.bfloat16)
    out_ref[:, columns:] = pieces(mine_ref[:, columns:] + whole(theirs_ref[:, columns:]))


def add(mine, theirs):
    return pl.pallas_call(
        add_kernel,
        out_shape=jax.ShapeDtypeStruct(theirs.shape, theirs.dtype),
        compiler_params=pltpu.CompilerParams(vmem_limit_bytes=VMEM_BYTES),
        name="add",
    )(mine, theirs)


def project(shifts, order, turns, weights):
    rows, width = turns[0].shape
    tokens = (rows - GAIN_ROWS) // XS
    columns = weights.shape[1]
    vmem = pl.BlockSpec(memory_space=pltpu.VMEM)
    return pl.pallas_call(
        functools.partial(project_kernel, shifts),
        out_shape=[
            jax.ShapeDtypeStruct((tokens, columns + HD), jnp.float32 if wide else jnp.bfloat16)
            for _, wide in shifts
        ],
        in_specs=[pl.BlockSpec(memory_space=pltpu.SMEM)]
        + [vmem] * 4
        + [pl.BlockSpec(memory_space=pltpu.HBM)],
        out_specs=[vmem] * len(shifts),
        scratch_shapes=[
            pltpu.VMEM((len(shifts) * tokens, columns), jnp.float32),
            pltpu.VMEM((len(shifts) * tokens, len(turns) * width), jnp.bfloat16),
            pltpu.VMEM(weights.shape, jnp.bfloat16),
            pltpu.VMEM((len(shifts) * tokens, HD), jnp.float32),
            pltpu.SemaphoreType.DMA((6,)),
        ],
        compiler_params=pltpu.CompilerParams(vmem_limit_bytes=VMEM_BYTES),
        cost_estimate=pl.CostEstimate(
            flops=64 * len(shifts) * tokens * weights.size,
            bytes_accessed=2 * weights.size,
            transcendentals=0,
        ),
        name="project",
    )(order, *turns, pltpu.with_memory_space_constraint(weights, pltpu.HBM))


def attend_kernel(length_ref, own_ref, p1, p2, out_ref):
    tokens, width = out_ref.shape
    columns = 3 * width
    total = own_ref[:, columns : columns + 1]
    for part in (p1, p2):
        total = total + whole(part[:, columns:])
    scale = lax.rsqrt(total / (8 * width) + 1e-06)
    length = length_ref[0]
    row = iota((tokens, tokens), 0)
    column = iota((tokens, tokens), 1)
    allowed = (column <= row) & (column < length)
    live = iota((tokens, HD), 0) < length
    for at in range(0, width, HD):
        query, keys, values = (
            (
                (
                    own_ref[:, a : a + HD]
                    + p1[:, a : a + HD].astype(jnp.float32)
                    + p2[:, a : a + HD].astype(jnp.float32)
                )
                * scale
            ).astype(jnp.bfloat16)
            for a in (at, width + at, 2 * width + at)
        )
        scores = lax.dot_general(
            query, keys, (((1,), (1,)), ((), ())), preferred_element_type=jnp.float32
        ) / math.sqrt(HD)
        scores = jnp.where(allowed, scores, jnp.float32(-1e30))
        powers = jnp.exp(scores - jnp.max(scores, axis=-1, keepdims=True))
        probs = (powers / jnp.sum(powers, axis=-1, keepdims=True)).astype(jnp.bfloat16)
        context = pick(probs, values)
        out_ref[:, at : at + HD] = jnp.where(live, context, 0.0).astype(jnp.bfloat16)


def attend(session_length, own, parts):
    tokens, columns = own.shape
    vmem = pl.BlockSpec(memory_space=pltpu.VMEM)
    return pl.pallas_call(
        attend_kernel,
        out_shape=jax.ShapeDtypeStruct((tokens, (columns - HD) // 3), jnp.bfloat16),
        in_specs=[pl.BlockSpec(memory_space=pltpu.SMEM)] + [vmem] * 3,
        out_specs=vmem,
        compiler_params=pltpu.CompilerParams(vmem_limit_bytes=VMEM_BYTES),
        name="attend",
    )(session_length, own, *parts)


def turn(value, axis, k):
    size = lax.axis_size(axis)
    return lax.ppermute(value, axis, [(i, (i + k) % size) for i in range(size)])


def exchange(value):
    return lax.all_to_all(value, DP, split_axis=0, concat_axis=0, tiled=True)


def local(
    session_length,
    event_owner,
    event_row,
    text_rows,
    image_rows,
    price,
    price_dir,
    norm_gain,
    w_query,
    w_key,
    w_value,
    cotangent,
):
    peers = lax.axis_size(DP)
    parts = lax.axis_size("mp")
    mine, across = lax.axis_index("mp"), lax.axis_index("x")
    tok_count = event_row.shape[0]
    capacity = 2 * tok_count // peers
    col_width = text_rows.shape[1]
    block = CS * w_query.shape[0]

    requests, codes, joint = request(event_owner, event_row, w_query, w_key, w_value)
    got_ids = exchange(requests)
    weights = lax.all_gather(joint, ("z", "c"), axis=0, tiled=True)
    table = join(text_rows, image_rows, price, price_dir)
    got_ids, table = lax.optimization_barrier((got_ids, table))
    replies, codes, norm_gain = lax.optimization_barrier(
        (answer(got_ids, table), codes, norm_gain)
    )
    packed = (peers, XS * capacity, col_width // XS)
    flat = (peers * XS * capacity, col_width // XS)
    replies = exchange(replies.reshape(packed)).reshape(flat)
    gain = lax.dynamic_index_in_dim(
        norm_gain.reshape(-1, XS, block), across, 1, keepdims=False
    ).reshape(1, -1)
    grads = pack(codes, cotangent)
    all_codes = lax.all_gather(codes, "x", axis=0, tiled=True)
    order = jnp.concatenate(
        [(mine - jnp.arange(parts, dtype=jnp.int32)) % parts, across[None]]
    ).astype(jnp.int32)
    replies, all_codes, gain, order, grads = lax.optimization_barrier(
        (replies, all_codes, gain, order, grads)
    )
    joined = select(all_codes, replies, gain)
    turns = [joined] + [turn(joined, "mp", k) for k in range(1, parts)]
    grads, _ = lax.optimization_barrier((grads, joined))
    got_grads = exchange(grads.reshape(packed)).reshape(flat)

    (far,) = project(((2, False),), order, turns, weights)
    far = turn(far, "x", 3)
    own, after, before = project(((0, True), (1, False), (3, True)), order, turns, weights)
    after = turn(after, "x", 1)
    before = turn(add(before, far), "x", 3)
    text_grad, image_grad = credit(got_ids, got_grads, text_rows, image_rows)
    context = attend(session_length, own, (after, before))
    return (context, text_grad, image_grad)


def solution(mesh):
    fine = Mesh(mesh.devices.reshape(-1, XS, CS, mesh.shape["mp"]), (*DP, "mp"))
    return jax.shard_map(
        local,
        mesh=fine,
        in_specs=(
            P(DP),
            P(DP, None),
            P(DP),
            P(DP, "mp"),
            P(DP, "mp"),
            P(DP),
            P("mp"),
            P("mp"),
            P(DP, "mp"),
            P(DP, "mp"),
            P(DP, "mp"),
            P(DP, "mp"),
        ),
        out_specs=(P(DP, "mp"), P(DP, "mp"), P(DP, "mp")),
        check_vma=False,
    )
```

```python
import functools
import math

import jax
import jax.numpy as jnp
from jax import lax
from jax.experimental import pallas as pl
from jax.experimental.pallas import tpu as pltpu
from jax.sharding import Mesh
from jax.sharding import PartitionSpec as P

HD = 128
GAIN_ROWS = 8
VMEM_BYTES = 24 * 1024 * 1024
XS = 4
CS = 2
DP = ("z", "x", "c")


def pick(selector, values):
    return jnp.dot(selector, values, preferred_element_type=jnp.float32)


def iota(shape, axis):
    return lax.broadcasted_iota(jnp.int32, shape, axis)


def turned(row):
    count = row.shape[1]
    diagonal = iota((count, count), 0) == iota((count, count), 1)
    return jnp.sum(jnp.where(diagonal, row.astype(jnp.float32), 0.0), axis=1, keepdims=True)


def request_kernel(owner_ref, row_ref, wq_ref, wk_ref, wv_ref, requests_ref, codes_ref, w_ref):
    count = owner_ref.shape[1]
    owner_row = owner_ref[...]
    owner_column = turned(owner_row).astype(jnp.int32)
    first, second = iota((count, count), 0), iota((count, count), 1)
    same = owner_row == owner_column
    earlier_column = jnp.sum(
        jnp.where(same & (second < first), 1.0, 0.0), axis=1, keepdims=True
    ).astype(jnp.int32)
    earlier_row = jnp.sum(
        jnp.where(same & (first < second), 1.0, 0.0), axis=0, keepdims=True
    ).astype(jnp.int32)
    asked = jnp.where(earlier_column == second, turned(row_ref[...]) + 1.0, 0.0)
    named = jnp.where(owner_row == first, 1.0, 0.0)
    found = pick(named.astype(jnp.bfloat16), asked.astype(jnp.bfloat16))
    requests_ref[...] = found.astype(jnp.int32) - 1
    codes_ref[...] = owner_row * (2 * XS) + earlier_row
    width = wq_ref.shape[1]
    for k, part in enumerate((wq_ref, wk_ref, wv_ref)):
        w_ref[:, k * width : (k + 1) * width] = part[...]


def request(event_owner, event_row, *projections):
    count = event_row.shape[0]
    depth, width = projections[0].shape
    return pl.pallas_call(
        request_kernel,
        out_shape=[
            jax.ShapeDtypeStruct((count, HD), jnp.int32),
            jax.ShapeDtypeStruct((1, count), jnp.int32),
            jax.ShapeDtypeStruct((depth, 3 * width), jnp.bfloat16),
        ],
        name="request",
    )(event_owner.reshape(1, count), event_row.reshape(1, count), *projections)


def join_kernel(text_ref, image_ref, price_ref, dir_ref, out_ref):
    columns = text_ref.shape[1]
    joined = (
        text_ref[...].astype(jnp.float32) * image_ref[...].astype(jnp.float32)
        + turned(price_ref[...]) * dir_ref[...].astype(jnp.float32)
    )
    width, depth = columns // XS, columns // XS // XS
    for x in range(XS):
        out_ref[:, x * width : (x + 1) * width] = jnp.concatenate(
            [joined[:, z * width + x * depth : z * width + (x + 1) * depth] for z in range(XS)],
            axis=1,
        ).astype(jnp.bfloat16)


def join(text_rows, image_rows, price, price_dir):
    return pl.pallas_call(
        join_kernel,
        out_shape=jax.ShapeDtypeStruct(text_rows.shape, jnp.bfloat16),
        compiler_params=pltpu.CompilerParams(vmem_limit_bytes=VMEM_BYTES),
        name="join",
    )(text_rows, image_rows, price.reshape(1, -1), price_dir.reshape(1, -1))


def answer_kernel(ids_ref, table_ref, out_ref):
    peers, table_rows = ids_ref.shape[0], table_ref.shape[0]
    count = 2 * peers
    width = table_ref.shape[1] // XS
    group = 2 * XS * CS
    target = iota((count, peers), 0)
    at = lax.rem(target, group)
    peer = (target - at) // 2 + lax.rem(at // 2, XS) * CS + at // (2 * XS)
    moved = jnp.where(peer == iota((count, peers), 1), 1.0, 0.0).astype(jnp.bfloat16)
    both = pick(moved, ids_ref[...].astype(jnp.float32).astype(jnp.bfloat16))
    lane, turn_of = iota(both.shape, 1), lax.rem(iota(both.shape, 0), 2)
    ids = jnp.sum(jnp.where(lane == turn_of, both, 0.0), axis=1, keepdims=True).astype(jnp.int32)
    wanted = jnp.where(ids == iota((count, table_rows), 1), 1.0, 0.0).astype(jnp.bfloat16)
    for block in range(XS):
        rows = pick(wanted, table_ref[:, block * width : (block + 1) * width]).astype(
            jnp.bfloat16
        )
        for z in range(count // group):
            to = (z * XS + block) * group
            out_ref[to : to + group, :] = rows[z * group : (z + 1) * group, :]


def answer(ids, table):
    return pl.pallas_call(
        answer_kernel,
        out_shape=jax.ShapeDtypeStruct(
            (2 * ids.shape[0] * XS, table.shape[1] // XS), jnp.bfloat16
        ),
        compiler_params=pltpu.CompilerParams(vmem_limit_bytes=VMEM_BYTES),
        name="answer",
    )(ids, table)


def select_kernel(codes_ref, replies_ref, gain_ref, out_ref):
    tokens, rows = codes_ref.shape[1], replies_ref.shape[0]
    replies = replies_ref[...]
    for x in range(XS):
        code = turned(codes_ref[x : x + 1, :]).astype(jnp.int32) + 2 * x
        chosen = jnp.where(code == iota((tokens, rows), 1), 1.0, 0.0).astype(jnp.bfloat16)
        out_ref[x * tokens : (x + 1) * tokens, :] = pick(chosen, replies).astype(jnp.bfloat16)
    out_ref[XS * tokens :, :] = jnp.broadcast_to(gain_ref[...], (GAIN_ROWS, gain_ref.shape[1]))


def select(codes, replies, gain):
    tokens, width = codes.size, replies.shape[1]
    return pl.pallas_call(
        select_kernel,
        out_shape=jax.ShapeDtypeStruct((tokens + GAIN_ROWS, width), jnp.bfloat16),
        compiler_params=pltpu.CompilerParams(vmem_limit_bytes=VMEM_BYTES),
        name="select",
    )(codes, replies, gain)


def pack_kernel(codes_ref, grads_ref, out_ref):
    rows, width = out_ref.shape
    tokens = codes_ref.shape[1]
    number = iota((rows, tokens), 0)
    code = number // (2 * XS) * (2 * XS) + lax.rem(number, 2 * XS) // XS
    block = lax.rem(number, XS)
    total = jnp.zeros((rows, width), jnp.float32)
    for q in range(XS):
        chosen = jnp.where((codes_ref[...] == code) & (block == q), 1.0, 0.0).astype(jnp.bfloat16)
        total = total + pick(chosen, grads_ref[:, q * width : (q + 1) * width])
    out_ref[...] = total.astype(jnp.bfloat16)


def pack(codes, grads):
    rows, width = 2 * XS * grads.shape[0], grads.shape[1] // XS
    return pl.pallas_call(
        pack_kernel,
        out_shape=jax.ShapeDtypeStruct((rows, width), jnp.bfloat16),
        compiler_params=pltpu.CompilerParams(vmem_limit_bytes=VMEM_BYTES),
        cost_estimate=pl.CostEstimate(
            flops=16 * rows * grads.size, bytes_accessed=2 * rows * width, transcendentals=0
        ),
        name="pack",
    )(codes, grads)


def name_kernel(ids_ref, out_ref):
    peers, rows = ids_ref.shape[0], out_ref.shape[1]
    spread = jnp.where(
        iota((peers, rows), 0) == iota((peers, rows), 1) // (2 * XS), 1.0, 0.0
    ).astype(jnp.bfloat16)
    both = lax.dot_general(
        ids_ref[...].astype(jnp.float32).astype(jnp.bfloat16),
        spread,
        (((0,), (0,)), ((), ())),
        preferred_element_type=jnp.float32,
    )
    turn_of = lax.rem(iota(both.shape, 1), 2 * XS) // XS
    ids = jnp.sum(jnp.where(iota(both.shape, 0) == turn_of, both, 0.0), axis=0, keepdims=True)
    out_ref[...] = ids.astype(jnp.int32)


def name(ids):
    return pl.pallas_call(
        name_kernel,
        out_shape=jax.ShapeDtypeStruct((1, 2 * XS * ids.shape[0]), jnp.int32),
        compiler_params=pltpu.CompilerParams(vmem_limit_bytes=VMEM_BYTES),
        name="name",
    )(ids)


def credit_kernel(named_ref, grads_ref, text_ref, image_ref, text_out, image_out):
    table_rows = text_ref.shape[0]
    rows, width = grads_ref.shape
    block = lax.rem(iota((1, rows), 1), XS)
    row = iota((table_rows, rows), 0)
    for q in range(XS):
        at = slice(q * width, (q + 1) * width)
        named = jnp.where(block == q, named_ref[...], -1)
        total = pick(jnp.where(row == named, 1.0, 0.0).astype(jnp.bfloat16), grads_ref[...])
        text_out[:, at] = total * image_ref[:, at].astype(jnp.float32)
        image_out[:, at] = total * text_ref[:, at].astype(jnp.float32)


def credit(named, grads, text_rows, image_rows):
    out = jax.ShapeDtypeStruct(text_rows.shape, jnp.float32)
    return pl.pallas_call(
        credit_kernel,
        out_shape=[out, out],
        compiler_params=pltpu.CompilerParams(vmem_limit_bytes=VMEM_BYTES),
        name="credit",
    )(
        named,
        grads,
        pltpu.with_memory_space_constraint(text_rows, pltpu.HBM),
        pltpu.with_memory_space_constraint(image_rows, pltpu.HBM),
    )


def project_kernel(shifts, order_ref, f0, f1, f2, f3, w_ref, *refs):
    outs, (acc_ref, normed_ref, held_ref, sum_ref, sem) = refs[: len(shifts)], refs[len(shifts) :]
    tokens = acc_ref.shape[0] // len(shifts)
    columns = acc_ref.shape[1]
    width = f0.shape[1]
    parts = (f0, f1, f2, f3)
    copies = []
    for k in range(len(parts)):
        there = pl.ds(pl.multiple_of(order_ref[k] * width, width), width)
        copies.append(
            pltpu.make_async_copy(
                w_ref.at[there, :], held_ref.at[k * width : (k + 1) * width, :], sem.at[k]
            )
        )
        copies[-1].start()

    mine = order_ref[XS]
    for n, shift in enumerate(shifts):
        rows = slice(n * tokens, (n + 1) * tokens)
        there = pl.ds(pl.multiple_of(lax.rem(mine + shift, XS) * tokens, tokens), tokens)
        total = jnp.zeros((tokens, 1), jnp.float32)
        for k, part in enumerate(parts):
            value = part[there, :].astype(jnp.float32)
            gain = part[XS * tokens : XS * tokens + 1, :].astype(jnp.float32)
            total = total + jnp.sum(value * value, axis=1, keepdims=True)
            normed_ref[rows, k * width : (k + 1) * width] = (value * gain).astype(jnp.bfloat16)
        sum_ref[rows, :] = jnp.broadcast_to(total, (tokens, HD))

    for copy in copies:
        copy.wait()
    tile = columns // 6
    for at in range(0, columns, tile):
        acc_ref[:, at : at + tile] = pick(normed_ref[...], held_ref[:, at : at + tile])

    lane = iota((tokens, HD), 1)
    for n, (shift, out_ref) in enumerate(zip(shifts, outs)):
        rows = slice(n * tokens, (n + 1) * tokens)
        total = sum_ref[rows, :]
        if shift == 0:
            out_ref[:, :columns] = acc_ref[rows, :]
            out_ref[:, columns:] = total
        else:
            out_ref[:, :columns] = acc_ref[rows, :].astype(jnp.bfloat16)
            high = total.astype(jnp.bfloat16).astype(jnp.float32)
            middle = (total - high).astype(jnp.bfloat16).astype(jnp.float32)
            low = total - high - middle
            out_ref[:, columns:] = jnp.where(
                lane == 0, high, jnp.where(lane == 1, middle, low)
            ).astype(jnp.bfloat16)


def project(shifts, order, turns, weights):
    rows, width = turns[0].shape
    tokens = (rows - GAIN_ROWS) // XS
    columns = weights.shape[1]
    vmem = pl.BlockSpec(memory_space=pltpu.VMEM)
    return pl.pallas_call(
        functools.partial(project_kernel, shifts),
        out_shape=[
            jax.ShapeDtypeStruct((tokens, columns + HD), jnp.bfloat16 if shift else jnp.float32)
            for shift in shifts
        ],
        in_specs=[pl.BlockSpec(memory_space=pltpu.SMEM)]
        + [vmem] * 4
        + [pl.BlockSpec(memory_space=pltpu.HBM)],
        out_specs=[vmem] * len(shifts),
        scratch_shapes=[
            pltpu.VMEM((len(shifts) * tokens, columns), jnp.float32),
            pltpu.VMEM((len(shifts) * tokens, len(turns) * width), jnp.bfloat16),
            pltpu.VMEM(weights.shape, jnp.bfloat16),
            pltpu.VMEM((len(shifts) * tokens, HD), jnp.float32),
            pltpu.SemaphoreType.DMA((len(turns),)),
        ],
        compiler_params=pltpu.CompilerParams(vmem_limit_bytes=VMEM_BYTES),
        cost_estimate=pl.CostEstimate(
            flops=64 * len(shifts) * tokens * weights.size,
            bytes_accessed=2 * weights.size,
            transcendentals=0,
        ),
        name="project",
    )(order, *turns, pltpu.with_memory_space_constraint(weights, pltpu.HBM))


def attend_kernel(length_ref, own_ref, p1, p2, p3, out_ref):
    tokens, width = out_ref.shape
    columns = 3 * width
    total = own_ref[:, columns : columns + 1]
    for part in (p1, p2, p3):
        pieces = part[:, columns : columns + HD].astype(jnp.float32)
        total = total + ((pieces[:, 0:1] + pieces[:, 1:2]) + pieces[:, 2:3])
    scale = lax.rsqrt(total / (8 * width) + 1e-06)
    length = length_ref[0]
    row = iota((tokens, tokens), 0)
    column = iota((tokens, tokens), 1)
    allowed = (column <= row) & (column < length)
    live = iota((tokens, HD), 0) < length
    for at in range(0, width, HD):
        query, keys, values = (
            (
                (
                    own_ref[:, a : a + HD]
                    + p1[:, a : a + HD].astype(jnp.float32)
                    + p2[:, a : a + HD].astype(jnp.float32)
                    + p3[:, a : a + HD].astype(jnp.float32)
                )
                * scale
            ).astype(jnp.bfloat16)
            for a in (at, width + at, 2 * width + at)
        )
        scores = lax.dot_general(
            query, keys, (((1,), (1,)), ((), ())), preferred_element_type=jnp.float32
        ) / math.sqrt(HD)
        scores = jnp.where(allowed, scores, jnp.float32(-1e30))
        powers = jnp.exp(scores - jnp.max(scores, axis=-1, keepdims=True))
        probs = (powers / jnp.sum(powers, axis=-1, keepdims=True)).astype(jnp.bfloat16)
        context = pick(probs, values)
        out_ref[:, at : at + HD] = jnp.where(live, context, 0.0).astype(jnp.bfloat16)


def attend(session_length, own, parts):
    tokens, columns = own.shape
    vmem = pl.BlockSpec(memory_space=pltpu.VMEM)
    return pl.pallas_call(
        attend_kernel,
        out_shape=jax.ShapeDtypeStruct((tokens, (columns - HD) // 3), jnp.bfloat16),
        in_specs=[pl.BlockSpec(memory_space=pltpu.SMEM)] + [vmem] * 4,
        out_specs=vmem,
        compiler_params=pltpu.CompilerParams(vmem_limit_bytes=VMEM_BYTES),
        name="attend",
    )(session_length, own, *parts)


def turn(value, axis, k):
    size = lax.axis_size(axis)
    return lax.ppermute(value, axis, [(i, (i + k) % size) for i in range(size)])


def exchange(value):
    return lax.all_to_all(value, DP, split_axis=0, concat_axis=0, tiled=True)


def local(
    session_length,
    event_owner,
    event_row,
    text_rows,
    image_rows,
    price,
    price_dir,
    norm_gain,
    w_query,
    w_key,
    w_value,
    cotangent,
):
    peers = lax.axis_size(DP)
    parts = lax.axis_size("mp")
    mine, across = lax.axis_index("mp"), lax.axis_index("x")
    tok_count = event_row.shape[0]
    capacity = 2 * tok_count // peers
    col_width = text_rows.shape[1]
    block = CS * w_query.shape[0]

    requests, codes, joint = request(event_owner, event_row, w_query, w_key, w_value)
    got_ids = exchange(requests)
    weights = lax.all_gather(joint, ("z", "c"), axis=0, tiled=True)
    table = join(text_rows, image_rows, price, price_dir)
    got_ids, table = lax.optimization_barrier((got_ids, table))
    replies, codes, norm_gain, got_ids = lax.optimization_barrier(
        (answer(got_ids, table), codes, norm_gain, got_ids)
    )
    packed = (peers, XS * capacity, col_width // XS)
    flat = (peers * XS * capacity, col_width // XS)
    replies = exchange(replies.reshape(packed)).reshape(flat)
    gain = lax.dynamic_index_in_dim(
        norm_gain.reshape(-1, XS, block), across, 1, keepdims=False
    ).reshape(1, -1)
    grads = pack(codes, cotangent)
    named = name(got_ids)
    all_codes = lax.all_gather(codes, "x", axis=0, tiled=True)
    order = jnp.concatenate(
        [(mine - jnp.arange(parts, dtype=jnp.int32)) % parts, across[None]]
    ).astype(jnp.int32)
    replies, all_codes, gain, order, grads, named = lax.optimization_barrier(
        (replies, all_codes, gain, order, grads, named)
    )
    joined = select(all_codes, replies, gain)
    turns = [joined] + [turn(joined, "mp", k) for k in range(1, parts)]
    grads, _ = lax.optimization_barrier((grads, joined))
    got_grads = exchange(grads.reshape(packed)).reshape(flat)

    (far,) = project((2,), order, turns, weights)
    own, after, before = project((0, 1, 3), order, turns, weights)
    far = turn(far, "x", 2)
    far, got_grads = lax.optimization_barrier((far, got_grads))
    received = (turn(after, "x", 1), far, turn(before, "x", 3))
    text_grad, image_grad = credit(named, got_grads, text_rows, image_rows)
    context = attend(session_length, own, received)
    return (context, text_grad, image_grad)


def solution(mesh):
    fine = Mesh(mesh.devices.reshape(-1, XS, CS, mesh.shape["mp"]), (*DP, "mp"))
    return jax.shard_map(
        local,
        mesh=fine,
        in_specs=(
            P(DP),
            P(DP, None),
            P(DP),
            P(DP, "mp"),
            P(DP, "mp"),
            P(DP),
            P("mp"),
            P("mp"),
            P(DP, "mp"),
            P(DP, "mp"),
            P(DP, "mp"),
            P(DP, "mp"),
        ),
        out_specs=(P(DP, "mp"), P(DP, "mp"), P(DP, "mp")),
        check_vma=False,
    )
```

```python
import functools
import math

import jax
import jax.numpy as jnp
from jax import lax
from jax.experimental import pallas as pl
from jax.experimental.pallas import tpu as pltpu
from jax.sharding import Mesh
from jax.sharding import PartitionSpec as P

HD = 128
GAIN_ROWS = 8
VMEM_BYTES = 24 * 1024 * 1024
XS = 4
CS = 2
DP = ("z", "x", "c")


def pick(selector, values):
    return jnp.dot(selector, values, preferred_element_type=jnp.float32)


def iota(shape, axis):
    return lax.broadcasted_iota(jnp.int32, shape, axis)


def turned(row):
    count = row.shape[1]
    diagonal = iota((count, count), 0) == iota((count, count), 1)
    return jnp.sum(jnp.where(diagonal, row.astype(jnp.float32), 0.0), axis=1, keepdims=True)


def request_kernel(owner_ref, row_ref, wq_ref, wk_ref, wv_ref, requests_ref, codes_ref, w_ref):
    count = owner_ref.shape[1]
    owner_row = owner_ref[...]
    owner_column = turned(owner_row).astype(jnp.int32)
    first, second = iota((count, count), 0), iota((count, count), 1)
    same = owner_row == owner_column
    earlier_column = jnp.sum(
        jnp.where(same & (second < first), 1.0, 0.0), axis=1, keepdims=True
    ).astype(jnp.int32)
    earlier_row = jnp.sum(
        jnp.where(same & (first < second), 1.0, 0.0), axis=0, keepdims=True
    ).astype(jnp.int32)
    asked = jnp.where(earlier_column == second, turned(row_ref[...]) + 1.0, 0.0)
    named = jnp.where(owner_row == first, 1.0, 0.0)
    found = pick(named.astype(jnp.bfloat16), asked.astype(jnp.bfloat16))
    requests_ref[...] = found.astype(jnp.int32) - 1
    codes_ref[...] = owner_row * (2 * XS) + earlier_row
    width = wq_ref.shape[1]
    for k, part in enumerate((wq_ref, wk_ref, wv_ref)):
        w_ref[:, k * width : (k + 1) * width] = part[...]


def request(event_owner, event_row, *projections):
    count = event_row.shape[0]
    depth, width = projections[0].shape
    return pl.pallas_call(
        request_kernel,
        out_shape=[
            jax.ShapeDtypeStruct((count, HD), jnp.int32),
            jax.ShapeDtypeStruct((1, count), jnp.int32),
            jax.ShapeDtypeStruct((depth, 3 * width), jnp.bfloat16),
        ],
        name="request",
    )(event_owner.reshape(1, count), event_row.reshape(1, count), *projections)


def join_kernel(text_ref, image_ref, price_ref, dir_ref, out_ref):
    columns = text_ref.shape[1]
    joined = (
        text_ref[...].astype(jnp.float32) * image_ref[...].astype(jnp.float32)
        + turned(price_ref[...]) * dir_ref[...].astype(jnp.float32)
    )
    width, depth = columns // XS, columns // XS // XS
    for x in range(XS):
        out_ref[:, x * width : (x + 1) * width] = jnp.concatenate(
            [joined[:, z * width + x * depth : z * width + (x + 1) * depth] for z in range(XS)],
            axis=1,
        ).astype(jnp.bfloat16)


def join(text_rows, image_rows, price, price_dir):
    return pl.pallas_call(
        join_kernel,
        out_shape=jax.ShapeDtypeStruct(text_rows.shape, jnp.bfloat16),
        compiler_params=pltpu.CompilerParams(vmem_limit_bytes=VMEM_BYTES),
        name="join",
    )(text_rows, image_rows, price.reshape(1, -1), price_dir.reshape(1, -1))


def answer_kernel(ids_ref, table_ref, out_ref):
    peers, table_rows = ids_ref.shape[0], table_ref.shape[0]
    count = 2 * peers
    width = table_ref.shape[1] // XS
    group = 2 * XS * CS
    target = iota((count, peers), 0)
    at = lax.rem(target, group)
    peer = (target - at) // 2 + lax.rem(at // 2, XS) * CS + at // (2 * XS)
    moved = jnp.where(peer == iota((count, peers), 1), 1.0, 0.0).astype(jnp.bfloat16)
    both = pick(moved, ids_ref[...].astype(jnp.float32).astype(jnp.bfloat16))
    lane, turn_of = iota(both.shape, 1), lax.rem(iota(both.shape, 0), 2)
    ids = jnp.sum(jnp.where(lane == turn_of, both, 0.0), axis=1, keepdims=True).astype(jnp.int32)
    wanted = jnp.where(ids == iota((count, table_rows), 1), 1.0, 0.0).astype(jnp.bfloat16)
    for block in range(XS):
        rows = pick(wanted, table_ref[:, block * width : (block + 1) * width]).astype(
            jnp.bfloat16
        )
        for z in range(count // group):
            to = (z * XS + block) * group
            out_ref[to : to + group, :] = rows[z * group : (z + 1) * group, :]


def answer(ids, table):
    return pl.pallas_call(
        answer_kernel,
        out_shape=jax.ShapeDtypeStruct(
            (2 * ids.shape[0] * XS, table.shape[1] // XS), jnp.bfloat16
        ),
        compiler_params=pltpu.CompilerParams(vmem_limit_bytes=VMEM_BYTES),
        name="answer",
    )(ids, table)


def select_kernel(codes_ref, replies_ref, gain_ref, out_ref):
    tokens, rows = codes_ref.shape[1], replies_ref.shape[0]
    replies = replies_ref[...]
    for x in range(XS):
        code = turned(codes_ref[x : x + 1, :]).astype(jnp.int32) + 2 * x
        chosen = jnp.where(code == iota((tokens, rows), 1), 1.0, 0.0).astype(jnp.bfloat16)
        out_ref[x * tokens : (x + 1) * tokens, :] = pick(chosen, replies).astype(jnp.bfloat16)
    out_ref[XS * tokens :, :] = jnp.broadcast_to(gain_ref[...], (GAIN_ROWS, gain_ref.shape[1]))


def select(codes, replies, gain):
    tokens, width = codes.size, replies.shape[1]
    return pl.pallas_call(
        select_kernel,
        out_shape=jax.ShapeDtypeStruct((tokens + GAIN_ROWS, width), jnp.bfloat16),
        compiler_params=pltpu.CompilerParams(vmem_limit_bytes=VMEM_BYTES),
        name="select",
    )(codes, replies, gain)


def pack_kernel(codes_ref, grads_ref, out_ref):
    rows, width = out_ref.shape
    tokens = codes_ref.shape[1]
    number = iota((rows, tokens), 0)
    code = number // (2 * XS) * (2 * XS) + lax.rem(number, 2 * XS) // XS
    block = lax.rem(number, XS)
    total = jnp.zeros((rows, width), jnp.float32)
    for q in range(XS):
        chosen = jnp.where((codes_ref[...] == code) & (block == q), 1.0, 0.0).astype(jnp.bfloat16)
        total = total + pick(chosen, grads_ref[:, q * width : (q + 1) * width])
    out_ref[...] = total.astype(jnp.bfloat16)


def pack(codes, grads):
    rows, width = 2 * XS * grads.shape[0], grads.shape[1] // XS
    return pl.pallas_call(
        pack_kernel,
        out_shape=jax.ShapeDtypeStruct((rows, width), jnp.bfloat16),
        compiler_params=pltpu.CompilerParams(vmem_limit_bytes=VMEM_BYTES),
        cost_estimate=pl.CostEstimate(
            flops=16 * rows * grads.size, bytes_accessed=2 * rows * width, transcendentals=0
        ),
        name="pack",
    )(codes, grads)


def name_kernel(ids_ref, out_ref):
    peers, rows = ids_ref.shape[0], out_ref.shape[1]
    spread = jnp.where(
        iota((peers, rows), 0) == iota((peers, rows), 1) // (2 * XS), 1.0, 0.0
    ).astype(jnp.bfloat16)
    both = lax.dot_general(
        ids_ref[...].astype(jnp.float32).astype(jnp.bfloat16),
        spread,
        (((0,), (0,)), ((), ())),
        preferred_element_type=jnp.float32,
    )
    turn_of = lax.rem(iota(both.shape, 1), 2 * XS) // XS
    ids = jnp.sum(jnp.where(iota(both.shape, 0) == turn_of, both, 0.0), axis=0, keepdims=True)
    out_ref[...] = ids.astype(jnp.int32)


def name(ids):
    return pl.pallas_call(
        name_kernel,
        out_shape=jax.ShapeDtypeStruct((1, 2 * XS * ids.shape[0]), jnp.int32),
        compiler_params=pltpu.CompilerParams(vmem_limit_bytes=VMEM_BYTES),
        name="name",
    )(ids)


def credit_kernel(named_ref, grads_ref, text_ref, image_ref, text_out, image_out):
    table_rows = text_ref.shape[0]
    rows, width = grads_ref.shape
    block = lax.rem(iota((1, rows), 1), XS)
    row = iota((table_rows, rows), 0)
    for q in range(XS):
        at = slice(q * width, (q + 1) * width)
        named = jnp.where(block == q, named_ref[...], -1)
        total = pick(jnp.where(row == named, 1.0, 0.0).astype(jnp.bfloat16), grads_ref[...])
        text_out[:, at] = total * image_ref[:, at].astype(jnp.float32)
        image_out[:, at] = total * text_ref[:, at].astype(jnp.float32)


def credit(named, grads, text_rows, image_rows):
    out = jax.ShapeDtypeStruct(text_rows.shape, jnp.float32)
    return pl.pallas_call(
        credit_kernel,
        out_shape=[out, out],
        compiler_params=pltpu.CompilerParams(vmem_limit_bytes=VMEM_BYTES),
        name="credit",
    )(named, grads, text_rows, image_rows)


def project_kernel(shifts, order_ref, f0, f1, f2, f3, w_ref, *refs):
    outs, (acc_ref, normed_ref, held_ref, sum_ref, sem) = refs[: len(shifts)], refs[len(shifts) :]
    tokens = acc_ref.shape[0] // len(shifts)
    columns = acc_ref.shape[1]
    width = f0.shape[1]
    parts = (f0, f1, f2, f3)
    copies = []
    for k in range(len(parts)):
        there = pl.ds(pl.multiple_of(order_ref[k] * width, width), width)
        copies.append(
            pltpu.make_async_copy(
                w_ref.at[there, :], held_ref.at[k * width : (k + 1) * width, :], sem.at[k]
            )
        )
        copies[-1].start()

    mine = order_ref[XS]
    for n, shift in enumerate(shifts):
        rows = slice(n * tokens, (n + 1) * tokens)
        there = pl.ds(pl.multiple_of(lax.rem(mine + shift, XS) * tokens, tokens), tokens)
        total = jnp.zeros((tokens, 1), jnp.float32)
        for k, part in enumerate(parts):
            value = part[there, :].astype(jnp.float32)
            gain = part[XS * tokens : XS * tokens + 1, :].astype(jnp.float32)
            total = total + jnp.sum(value * value, axis=1, keepdims=True)
            normed_ref[rows, k * width : (k + 1) * width] = (value * gain).astype(jnp.bfloat16)
        sum_ref[rows, :] = jnp.broadcast_to(total, (tokens, HD))

    for copy in copies:
        copy.wait()
    tile = columns // 6
    for at in range(0, columns, tile):
        acc_ref[:, at : at + tile] = pick(normed_ref[...], held_ref[:, at : at + tile])

    lane = iota((tokens, HD), 1)
    for n, (shift, out_ref) in enumerate(zip(shifts, outs)):
        rows = slice(n * tokens, (n + 1) * tokens)
        total = sum_ref[rows, :]
        if shift == 0:
            out_ref[:, :columns] = acc_ref[rows, :]
            out_ref[:, columns:] = total
        else:
            out_ref[:, :columns] = acc_ref[rows, :].astype(jnp.bfloat16)
            high = total.astype(jnp.bfloat16).astype(jnp.float32)
            middle = (total - high).astype(jnp.bfloat16).astype(jnp.float32)
            low = total - high - middle
            out_ref[:, columns:] = jnp.where(
                lane == 0, high, jnp.where(lane == 1, middle, low)
            ).astype(jnp.bfloat16)


def project(shifts, order, turns, weights):
    rows, width = turns[0].shape
    tokens = (rows - GAIN_ROWS) // XS
    columns = weights.shape[1]
    vmem = pl.BlockSpec(memory_space=pltpu.VMEM)
    return pl.pallas_call(
        functools.partial(project_kernel, shifts),
        out_shape=[
            jax.ShapeDtypeStruct((tokens, columns + HD), jnp.bfloat16 if shift else jnp.float32)
            for shift in shifts
        ],
        in_specs=[pl.BlockSpec(memory_space=pltpu.SMEM)]
        + [vmem] * 4
        + [pl.BlockSpec(memory_space=pltpu.HBM)],
        out_specs=[vmem] * len(shifts),
        scratch_shapes=[
            pltpu.VMEM((len(shifts) * tokens, columns), jnp.float32),
            pltpu.VMEM((len(shifts) * tokens, len(turns) * width), jnp.bfloat16),
            pltpu.VMEM(weights.shape, jnp.bfloat16),
            pltpu.VMEM((len(shifts) * tokens, HD), jnp.float32),
            pltpu.SemaphoreType.DMA((len(turns),)),
        ],
        compiler_params=pltpu.CompilerParams(vmem_limit_bytes=VMEM_BYTES),
        cost_estimate=pl.CostEstimate(
            flops=64 * len(shifts) * tokens * weights.size,
            bytes_accessed=2 * weights.size,
            transcendentals=0,
        ),
        name="project",
    )(order, *turns, pltpu.with_memory_space_constraint(weights, pltpu.HBM))


def attend_kernel(length_ref, own_ref, p1, p2, p3, out_ref):
    tokens, width = out_ref.shape
    columns = 3 * width
    total = own_ref[:, columns : columns + 1]
    for part in (p1, p2, p3):
        pieces = part[:, columns : columns + HD].astype(jnp.float32)
        total = total + ((pieces[:, 0:1] + pieces[:, 1:2]) + pieces[:, 2:3])
    scale = lax.rsqrt(total / (8 * width) + 1e-06)
    length = length_ref[0]
    row = iota((tokens, tokens), 0)
    column = iota((tokens, tokens), 1)
    allowed = (column <= row) & (column < length)
    live = iota((tokens, HD), 0) < length
    for at in range(0, width, HD):
        query, keys, values = (
            (
                (
                    own_ref[:, a : a + HD]
                    + p1[:, a : a + HD].astype(jnp.float32)
                    + p2[:, a : a + HD].astype(jnp.float32)
                    + p3[:, a : a + HD].astype(jnp.float32)
                )
                * scale
            ).astype(jnp.bfloat16)
            for a in (at, width + at, 2 * width + at)
        )
        scores = lax.dot_general(
            query, keys, (((1,), (1,)), ((), ())), preferred_element_type=jnp.float32
        ) / math.sqrt(HD)
        scores = jnp.where(allowed, scores, jnp.float32(-1e30))
        powers = jnp.exp(scores - jnp.max(scores, axis=-1, keepdims=True))
        probs = (powers / jnp.sum(powers, axis=-1, keepdims=True)).astype(jnp.bfloat16)
        context = pick(probs, values)
        out_ref[:, at : at + HD] = jnp.where(live, context, 0.0).astype(jnp.bfloat16)


def attend(session_length, own, parts):
    tokens, columns = own.shape
    vmem = pl.BlockSpec(memory_space=pltpu.VMEM)
    return pl.pallas_call(
        attend_kernel,
        out_shape=jax.ShapeDtypeStruct((tokens, (columns - HD) // 3), jnp.bfloat16),
        in_specs=[pl.BlockSpec(memory_space=pltpu.SMEM)] + [vmem] * 4,
        out_specs=vmem,
        compiler_params=pltpu.CompilerParams(vmem_limit_bytes=VMEM_BYTES),
        name="attend",
    )(session_length, own, *parts)


def turn(value, axis, k):
    size = lax.axis_size(axis)
    return lax.ppermute(value, axis, [(i, (i + k) % size) for i in range(size)])


def exchange(value):
    return lax.all_to_all(value, DP, split_axis=0, concat_axis=0, tiled=True)


def local(
    session_length,
    event_owner,
    event_row,
    text_rows,
    image_rows,
    price,
    price_dir,
    norm_gain,
    w_query,
    w_key,
    w_value,
    cotangent,
):
    peers = lax.axis_size(DP)
    parts = lax.axis_size("mp")
    mine, across = lax.axis_index("mp"), lax.axis_index("x")
    tok_count = event_row.shape[0]
    capacity = 2 * tok_count // peers
    col_width = text_rows.shape[1]
    block = CS * w_query.shape[0]

    requests, codes, joint = request(event_owner, event_row, w_query, w_key, w_value)
    got_ids = exchange(requests)
    weights = lax.all_gather(joint, ("z", "c"), axis=0, tiled=True)
    table = join(text_rows, image_rows, price, price_dir)
    got_ids, table = lax.optimization_barrier((got_ids, table))
    replies, codes, norm_gain, got_ids = lax.optimization_barrier(
        (answer(got_ids, table), codes, norm_gain, got_ids)
    )
    packed = (peers, XS * capacity, col_width // XS)
    flat = (peers * XS * capacity, col_width // XS)
    replies = exchange(replies.reshape(packed)).reshape(flat)
    gain = lax.dynamic_index_in_dim(
        norm_gain.reshape(-1, XS, block), across, 1, keepdims=False
    ).reshape(1, -1)
    grads = pack(codes, cotangent)
    named = name(got_ids)
    all_codes = lax.all_gather(codes, "x", axis=0, tiled=True)
    order = jnp.concatenate(
        [(mine - jnp.arange(parts, dtype=jnp.int32)) % parts, across[None]]
    ).astype(jnp.int32)
    replies, all_codes, gain, order, grads, named = lax.optimization_barrier(
        (replies, all_codes, gain, order, grads, named)
    )
    joined = select(all_codes, replies, gain)
    turns = [joined] + [turn(joined, "mp", k) for k in range(1, parts)]
    grads, _ = lax.optimization_barrier((grads, joined))
    got_grads = exchange(grads.reshape(packed)).reshape(flat)

    (far,) = project((2,), order, turns, weights)
    own, after, before = project((0, 1, 3), order, turns, weights)
    far = turn(far, "x", 2)
    far, got_grads = lax.optimization_barrier((far, got_grads))
    received = (turn(after, "x", 1), far, turn(before, "x", 3))
    text_grad, image_grad = credit(named, got_grads, text_rows, image_rows)
    context = attend(session_length, own, received)
    return (context, text_grad, image_grad)


def solution(mesh):
    fine = Mesh(mesh.devices.reshape(-1, XS, CS, mesh.shape["mp"]), (*DP, "mp"))
    return jax.shard_map(
        local,
        mesh=fine,
        in_specs=(
            P(DP),
            P(DP, None),
            P(DP),
            P(DP, "mp"),
            P(DP, "mp"),
            P(DP),
            P("mp"),
            P("mp"),
            P(DP, "mp"),
            P(DP, "mp"),
            P(DP, "mp"),
            P(DP, "mp"),
        ),
        out_specs=(P(DP, "mp"), P(DP, "mp"), P(DP, "mp")),
        check_vma=False,
    )
```

```python
import functools
import math

import jax
import jax.numpy as jnp
from jax import lax
from jax.experimental import pallas as pl
from jax.experimental.pallas import tpu as pltpu
from jax.sharding import Mesh
from jax.sharding import PartitionSpec as P

HD = 128
GAIN_ROWS = 8
VMEM_BYTES = 24 * 1024 * 1024
XS = 4
CS = 2
DP = ("z", "x", "c")


def pick(selector, values):
    return jnp.dot(selector, values, preferred_element_type=jnp.float32)


def iota(shape, axis):
    return lax.broadcasted_iota(jnp.int32, shape, axis)


def turned(row):
    count = row.shape[1]
    diagonal = iota((count, count), 0) == iota((count, count), 1)
    return jnp.sum(jnp.where(diagonal, row.astype(jnp.float32), 0.0), axis=1, keepdims=True)


def request_kernel(owner_ref, row_ref, wq_ref, wk_ref, wv_ref, requests_ref, codes_ref, w_ref):
    count = owner_ref.shape[1]
    owner_row = owner_ref[...]
    owner_column = turned(owner_row).astype(jnp.int32)
    first, second = iota((count, count), 0), iota((count, count), 1)
    same = owner_row == owner_column
    earlier_column = jnp.sum(
        jnp.where(same & (second < first), 1.0, 0.0), axis=1, keepdims=True
    ).astype(jnp.int32)
    earlier_row = jnp.sum(
        jnp.where(same & (first < second), 1.0, 0.0), axis=0, keepdims=True
    ).astype(jnp.int32)
    asked = jnp.where(earlier_column == second, turned(row_ref[...]) + 1.0, 0.0)
    named = jnp.where(owner_row == first, 1.0, 0.0)
    found = pick(named.astype(jnp.bfloat16), asked.astype(jnp.bfloat16))
    requests_ref[...] = found.astype(jnp.int32) - 1
    codes_ref[...] = owner_row * (2 * XS) + earlier_row
    width = wq_ref.shape[1]
    for k, part in enumerate((wq_ref, wk_ref, wv_ref)):
        w_ref[:, k * width : (k + 1) * width] = part[...]


def request(event_owner, event_row, *projections):
    count = event_row.shape[0]
    depth, width = projections[0].shape
    return pl.pallas_call(
        request_kernel,
        out_shape=[
            jax.ShapeDtypeStruct((count, HD), jnp.int32),
            jax.ShapeDtypeStruct((1, count), jnp.int32),
            jax.ShapeDtypeStruct((depth, 3 * width), jnp.bfloat16),
        ],
        name="request",
    )(event_owner.reshape(1, count), event_row.reshape(1, count), *projections)


def join_kernel(text_ref, image_ref, price_ref, dir_ref, out_ref):
    columns = text_ref.shape[1]
    joined = (
        text_ref[...].astype(jnp.float32) * image_ref[...].astype(jnp.float32)
        + turned(price_ref[...]) * dir_ref[...].astype(jnp.float32)
    )
    width, depth = columns // XS, columns // XS // XS
    for x in range(XS):
        out_ref[:, x * width : (x + 1) * width] = jnp.concatenate(
            [joined[:, z * width + x * depth : z * width + (x + 1) * depth] for z in range(XS)],
            axis=1,
        ).astype(jnp.bfloat16)


def join(text_rows, image_rows, price, price_dir):
    return pl.pallas_call(
        join_kernel,
        out_shape=jax.ShapeDtypeStruct(text_rows.shape, jnp.bfloat16),
        compiler_params=pltpu.CompilerParams(vmem_limit_bytes=VMEM_BYTES),
        name="join",
    )(text_rows, image_rows, price.reshape(1, -1), price_dir.reshape(1, -1))


def answer_kernel(ids_ref, table_ref, out_ref):
    peers, table_rows = ids_ref.shape[0], table_ref.shape[0]
    count = 2 * peers
    width = table_ref.shape[1] // XS
    group = 2 * XS * CS
    target = iota((count, peers), 0)
    at = lax.rem(target, group)
    peer = (target - at) // 2 + lax.rem(at // 2, XS) * CS + at // (2 * XS)
    moved = jnp.where(peer == iota((count, peers), 1), 1.0, 0.0).astype(jnp.bfloat16)
    both = pick(moved, ids_ref[...].astype(jnp.float32).astype(jnp.bfloat16))
    lane, turn_of = iota(both.shape, 1), lax.rem(iota(both.shape, 0), 2)
    ids = jnp.sum(jnp.where(lane == turn_of, both, 0.0), axis=1, keepdims=True).astype(jnp.int32)
    wanted = jnp.where(ids == iota((count, table_rows), 1), 1.0, 0.0).astype(jnp.bfloat16)
    for block in range(XS):
        rows = pick(wanted, table_ref[:, block * width : (block + 1) * width]).astype(
            jnp.bfloat16
        )
        for z in range(count // group):
            to = (z * XS + block) * group
            out_ref[to : to + group, :] = rows[z * group : (z + 1) * group, :]


def answer(ids, table):
    return pl.pallas_call(
        answer_kernel,
        out_shape=jax.ShapeDtypeStruct(
            (2 * ids.shape[0] * XS, table.shape[1] // XS), jnp.bfloat16
        ),
        compiler_params=pltpu.CompilerParams(vmem_limit_bytes=VMEM_BYTES),
        name="answer",
    )(ids, table)


def select_kernel(codes_ref, replies_ref, gain_ref, out_ref):
    tokens, rows = codes_ref.shape[1], replies_ref.shape[0]
    replies = replies_ref[...]
    for x in range(XS):
        code = turned(codes_ref[x : x + 1, :]).astype(jnp.int32) + 2 * x
        chosen = jnp.where(code == iota((tokens, rows), 1), 1.0, 0.0).astype(jnp.bfloat16)
        out_ref[x * tokens : (x + 1) * tokens, :] = pick(chosen, replies).astype(jnp.bfloat16)
    out_ref[XS * tokens :, :] = jnp.broadcast_to(gain_ref[...], (GAIN_ROWS, gain_ref.shape[1]))


def select(codes, replies, gain):
    tokens, width = codes.size, replies.shape[1]
    return pl.pallas_call(
        select_kernel,
        out_shape=jax.ShapeDtypeStruct((tokens + GAIN_ROWS, width), jnp.bfloat16),
        compiler_params=pltpu.CompilerParams(vmem_limit_bytes=VMEM_BYTES),
        name="select",
    )(codes, replies, gain)


def pack_kernel(codes_ref, grads_ref, out_ref):
    rows, width = out_ref.shape
    tokens = codes_ref.shape[1]
    number = iota((rows, tokens), 0)
    code = number // (2 * XS) * (2 * XS) + lax.rem(number, 2 * XS) // XS
    block = lax.rem(number, XS)
    total = jnp.zeros((rows, width), jnp.float32)
    for q in range(XS):
        chosen = jnp.where((codes_ref[...] == code) & (block == q), 1.0, 0.0).astype(jnp.bfloat16)
        total = total + pick(chosen, grads_ref[:, q * width : (q + 1) * width])
    out_ref[...] = total.astype(jnp.bfloat16)


def pack(codes, grads):
    rows, width = 2 * XS * grads.shape[0], grads.shape[1] // XS
    return pl.pallas_call(
        pack_kernel,
        out_shape=jax.ShapeDtypeStruct((rows, width), jnp.bfloat16),
        compiler_params=pltpu.CompilerParams(vmem_limit_bytes=VMEM_BYTES),
        cost_estimate=pl.CostEstimate(
            flops=16 * rows * grads.size, bytes_accessed=2 * rows * width, transcendentals=0
        ),
        name="pack",
    )(codes, grads)


def name_kernel(ids_ref, out_ref):
    peers, rows = ids_ref.shape[0], out_ref.shape[1]
    spread = jnp.where(
        iota((peers, rows), 0) == iota((peers, rows), 1) // (2 * XS), 1.0, 0.0
    ).astype(jnp.bfloat16)
    both = lax.dot_general(
        ids_ref[...].astype(jnp.float32).astype(jnp.bfloat16),
        spread,
        (((0,), (0,)), ((), ())),
        preferred_element_type=jnp.float32,
    )
    turn_of = lax.rem(iota(both.shape, 1), 2 * XS) // XS
    ids = jnp.sum(jnp.where(iota(both.shape, 0) == turn_of, both, 0.0), axis=0, keepdims=True)
    out_ref[...] = ids.astype(jnp.int32)


def name(ids):
    return pl.pallas_call(
        name_kernel,
        out_shape=jax.ShapeDtypeStruct((1, 2 * XS * ids.shape[0]), jnp.int32),
        compiler_params=pltpu.CompilerParams(vmem_limit_bytes=VMEM_BYTES),
        name="name",
    )(ids)


def credit_kernel(named_ref, grads_ref, text_ref, image_ref, text_out, image_out):
    table_rows = text_ref.shape[0]
    rows, width = grads_ref.shape
    block = lax.rem(iota((1, rows), 1), XS)
    row = iota((table_rows, rows), 0)
    for q in range(XS):
        at = slice(q * width, (q + 1) * width)
        named = jnp.where(block == q, named_ref[...], -1)
        total = pick(jnp.where(row == named, 1.0, 0.0).astype(jnp.bfloat16), grads_ref[...])
        text_out[:, at] = total * image_ref[:, at].astype(jnp.float32)
        image_out[:, at] = total * text_ref[:, at].astype(jnp.float32)


def credit(named, grads, text_rows, image_rows):
    out = jax.ShapeDtypeStruct(text_rows.shape, jnp.float32)
    return pl.pallas_call(
        credit_kernel,
        out_shape=[out, out],
        compiler_params=pltpu.CompilerParams(vmem_limit_bytes=VMEM_BYTES),
        name="credit",
    )(named, grads, text_rows, image_rows)


def project_kernel(shifts, order_ref, f0, f1, f2, f3, w_ref, *refs):
    outs, (acc_ref, normed_ref, held_ref, sum_ref, sem) = refs[: len(shifts)], refs[len(shifts) :]
    tokens = acc_ref.shape[0] // len(shifts)
    columns = acc_ref.shape[1]
    width = f0.shape[1]
    parts = (f0, f1, f2, f3)
    copies = []
    for k in range(len(parts)):
        there = pl.ds(pl.multiple_of(order_ref[k] * width, width), width)
        copies.append(
            pltpu.make_async_copy(
                w_ref.at[there, :], held_ref.at[k * width : (k + 1) * width, :], sem.at[k]
            )
        )
        copies[-1].start()

    mine = order_ref[XS]
    for n, shift in enumerate(shifts):
        rows = slice(n * tokens, (n + 1) * tokens)
        there = pl.ds(pl.multiple_of(lax.rem(mine + shift, XS) * tokens, tokens), tokens)
        total = jnp.zeros((tokens, 1), jnp.float32)
        for k, part in enumerate(parts):
            value = part[there, :].astype(jnp.float32)
            gain = part[XS * tokens : XS * tokens + 1, :].astype(jnp.float32)
            total = total + jnp.sum(value * value, axis=1, keepdims=True)
            normed_ref[rows, k * width : (k + 1) * width] = (value * gain).astype(jnp.bfloat16)
        sum_ref[rows, :] = jnp.broadcast_to(total, (tokens, HD))

    for copy in copies:
        copy.wait()
    tile = columns // 6
    for at in range(0, columns, tile):
        acc_ref[:, at : at + tile] = pick(normed_ref[...], held_ref[:, at : at + tile])

    lane = iota((tokens, HD), 1)
    for n, (shift, out_ref) in enumerate(zip(shifts, outs)):
        rows = slice(n * tokens, (n + 1) * tokens)
        total = sum_ref[rows, :]
        if shift == 0:
            out_ref[:, :columns] = acc_ref[rows, :]
            out_ref[:, columns:] = total
        else:
            out_ref[:, :columns] = acc_ref[rows, :].astype(jnp.bfloat16)
            high = total.astype(jnp.bfloat16).astype(jnp.float32)
            middle = (total - high).astype(jnp.bfloat16).astype(jnp.float32)
            low = total - high - middle
            out_ref[:, columns:] = jnp.where(
                lane == 0, high, jnp.where(lane == 1, middle, low)
            ).astype(jnp.bfloat16)


def project(shifts, order, turns, weights):
    rows, width = turns[0].shape
    tokens = (rows - GAIN_ROWS) // XS
    columns = weights.shape[1]
    vmem = pl.BlockSpec(memory_space=pltpu.VMEM)
    return pl.pallas_call(
        functools.partial(project_kernel, shifts),
        out_shape=[
            jax.ShapeDtypeStruct((tokens, columns + HD), jnp.bfloat16 if shift else jnp.float32)
            for shift in shifts
        ],
        in_specs=[pl.BlockSpec(memory_space=pltpu.SMEM)]
        + [vmem] * 4
        + [pl.BlockSpec(memory_space=pltpu.HBM)],
        out_specs=[vmem] * len(shifts),
        scratch_shapes=[
            pltpu.VMEM((len(shifts) * tokens, columns), jnp.float32),
            pltpu.VMEM((len(shifts) * tokens, len(turns) * width), jnp.bfloat16),
            pltpu.VMEM(weights.shape, jnp.bfloat16),
            pltpu.VMEM((len(shifts) * tokens, HD), jnp.float32),
            pltpu.SemaphoreType.DMA((len(turns),)),
        ],
        compiler_params=pltpu.CompilerParams(vmem_limit_bytes=VMEM_BYTES),
        cost_estimate=pl.CostEstimate(
            flops=64 * len(shifts) * tokens * weights.size,
            bytes_accessed=2 * weights.size,
            transcendentals=0,
        ),
        name="project",
    )(order, *turns, pltpu.with_memory_space_constraint(weights, pltpu.HBM))


def attend_kernel(length_ref, own_ref, p1, p2, p3, out_ref):
    tokens, width = out_ref.shape
    columns = 3 * width
    total = own_ref[:, columns : columns + 1]
    for part in (p1, p2, p3):
        pieces = part[:, columns : columns + HD].astype(jnp.float32)
        total = total + ((pieces[:, 0:1] + pieces[:, 1:2]) + pieces[:, 2:3])
    scale = lax.rsqrt(total / (8 * width) + 1e-06)
    length = length_ref[0]
    row = iota((tokens, tokens), 0)
    column = iota((tokens, tokens), 1)
    allowed = (column <= row) & (column < length)
    live = iota((tokens, HD), 0) < length
    for at in range(0, width, HD):
        query, keys, values = (
            (
                (
                    own_ref[:, a : a + HD]
                    + p1[:, a : a + HD].astype(jnp.float32)
                    + p2[:, a : a + HD].astype(jnp.float32)
                    + p3[:, a : a + HD].astype(jnp.float32)
                )
                * scale
            ).astype(jnp.bfloat16)
            for a in (at, width + at, 2 * width + at)
        )
        scores = lax.dot_general(
            query, keys, (((1,), (1,)), ((), ())), preferred_element_type=jnp.float32
        ) / math.sqrt(HD)
        scores = jnp.where(allowed, scores, jnp.float32(-1e30))
        powers = jnp.exp(scores - jnp.max(scores, axis=-1, keepdims=True))
        probs = (powers / jnp.sum(powers, axis=-1, keepdims=True)).astype(jnp.bfloat16)
        context = pick(probs, values)
        out_ref[:, at : at + HD] = jnp.where(live, context, 0.0).astype(jnp.bfloat16)


def attend(session_length, own, parts):
    tokens, columns = own.shape
    vmem = pl.BlockSpec(memory_space=pltpu.VMEM)
    return pl.pallas_call(
        attend_kernel,
        out_shape=jax.ShapeDtypeStruct((tokens, (columns - HD) // 3), jnp.bfloat16),
        in_specs=[pl.BlockSpec(memory_space=pltpu.SMEM)] + [vmem] * 4,
        out_specs=vmem,
        compiler_params=pltpu.CompilerParams(vmem_limit_bytes=VMEM_BYTES),
        name="attend",
    )(session_length, own, *parts)


def turn(value, axis, k):
    size = lax.axis_size(axis)
    return lax.ppermute(value, axis, [(i, (i + k) % size) for i in range(size)])


def exchange(value):
    return lax.all_to_all(value, DP, split_axis=0, concat_axis=0, tiled=True)


def local(
    session_length,
    event_owner,
    event_row,
    text_rows,
    image_rows,
    price,
    price_dir,
    norm_gain,
    w_query,
    w_key,
    w_value,
    cotangent,
):
    peers = lax.axis_size(DP)
    parts = lax.axis_size("mp")
    mine, across = lax.axis_index("mp"), lax.axis_index("x")
    tok_count = event_row.shape[0]
    capacity = 2 * tok_count // peers
    col_width = text_rows.shape[1]
    block = CS * w_query.shape[0]

    requests, codes, joint = request(event_owner, event_row, w_query, w_key, w_value)
    got_ids = exchange(requests)
    weights = lax.all_gather(joint, ("z", "c"), axis=0, tiled=True)
    table = join(text_rows, image_rows, price, price_dir)
    got_ids, table = lax.optimization_barrier((got_ids, table))
    replies, codes, norm_gain, got_ids = lax.optimization_barrier(
        (answer(got_ids, table), codes, norm_gain, got_ids)
    )
    packed = (peers, XS * capacity, col_width // XS)
    flat = (peers * XS * capacity, col_width // XS)
    replies = exchange(replies.reshape(packed)).reshape(flat)
    gain = lax.dynamic_index_in_dim(
        norm_gain.reshape(-1, XS, block), across, 1, keepdims=False
    ).reshape(1, -1)
    grads = pack(codes, cotangent)
    named = name(got_ids)
    all_codes = lax.all_gather(codes, "x", axis=0, tiled=True)
    order = jnp.concatenate(
        [(mine - jnp.arange(parts, dtype=jnp.int32)) % parts, across[None]]
    ).astype(jnp.int32)
    replies, all_codes, gain, order, grads, named = lax.optimization_barrier(
        (replies, all_codes, gain, order, grads, named)
    )
    joined = select(all_codes, replies, gain)
    turns = [joined] + [turn(joined, "mp", k) for k in range(1, parts)]
    grads, _ = lax.optimization_barrier((grads, joined))
    got_grads = exchange(grads.reshape(packed)).reshape(flat)

    (far,) = project((2,), order, turns, weights)
    own, after, before = project((0, 1, 3), order, turns, weights)
    received = (turn(after, "x", 1), turn(far, "x", 2), turn(before, "x", 3))
    context = attend(session_length, own, received)
    context, got_grads = lax.optimization_barrier((context, got_grads))
    text_grad, image_grad = credit(named, got_grads, text_rows, image_rows)
    return (context, text_grad, image_grad)


def solution(mesh):
    fine = Mesh(mesh.devices.reshape(-1, XS, CS, mesh.shape["mp"]), (*DP, "mp"))
    return jax.shard_map(
        local,
        mesh=fine,
        in_specs=(
            P(DP),
            P(DP, None),
            P(DP),
            P(DP, "mp"),
            P(DP, "mp"),
            P(DP),
            P("mp"),
            P("mp"),
            P(DP, "mp"),
            P(DP, "mp"),
            P(DP, "mp"),
            P(DP, "mp"),
        ),
        out_specs=(P(DP, "mp"), P(DP, "mp"), P(DP, "mp")),
        check_vma=False,
    )
```
